32 devices in a mesh: ctx: 8 (over z, x), head: 4 (over y, core).
Axes of the slice: x: 2, y: 2, z: 4, core: 2. Of those that a mesh axis runs over, the one named last changes fastest.
Arguments:
- span_query: bfloat16 [2048, 16384], P('ctx', 'head'), may hold values from -5 to 5
- span_key: bfloat16 [2048, 1024], P('ctx', 'head'), may hold values from -12 to 12
- span_value: bfloat16 [2048, 1024], P('ctx', 'head'), may hold values from -6 to 6
- block_lists: int32 [16, 6], replicated, may hold values from 0 to 15, all different within a row
- owners: int32 [16], replicated, may hold values from 0 to 7, as said below
- cache_key: bfloat16 [32768, 1024], P('ctx', 'head'), may hold values from -12 to 12
- cache_value: bfloat16 [32768, 1024], P('ctx', 'head'), may hold values from -6 to 6
- sample_query: bfloat16 [64, 16384], P(None, 'head'), may hold values from -5 to 5
- sample_key: bfloat16 [64, 1024], P(None, 'head'), may hold values from -24 to 24
- sample_value: bfloat16 [64, 1024], P(None, 'head'), may hold values from -6 to 6
- out_weight: bfloat16 [16384, 16384], P('head', 'ctx'), may hold values from -0.046875 to 0.046875
Outputs:
- span_out: bfloat16 [2048, 16384], P('ctx', 'head')
- sample_out: bfloat16 [64, 16384], P(None, 'ctx')
- appended_key: bfloat16 [8192, 1024], P('ctx', 'head')
- appended_value: bfloat16 [8192, 1024], P('ctx', 'head')
The draws below stay inside these ranges and needn't reach their ends.
Inputs may be any that keep to these rules, and one draw needn't show every extreme that they name: `block_lists`: each row lists 6 different key blocks. `owners`: no owner has more than 8 blocks, and some owner has exactly 8.
All inputs are finite; a program needn't handle non-finite values.
Results may differ from the reference program's by a relative error of at most 0.00245.
The reference program's roundings to bfloat16 on the way count: a program that leaves them out, or rounds other values in their place, can miss the bound.
Values may be sent and summed in bfloat16 or wider, within the bound.
A program may use at most 128 MiB of HBM per device.

```python
import jax
import jax.numpy as jnp
from jax import lax

D = 16384
QH = 128
KVH = 8
HD = 128
BLOCK = 128
KSEL = 6
RES_DEV = 4096
SAMPLES = 64
QBLK = 2
MOST_BLOCKS = 8
SPAN = 2048
NBLK = 16
RESIDENT = 32768
N_CTX = 8


def draw_span_key(key, part):
    base = jnp.clip(jax.random.normal(jax.random.fold_in(key, 11), (SPAN, KVH * HD), jnp.float32) * 2.5, -12.0, 12.0)
    return base.astype(jnp.bfloat16)


def draw_span_query(key, part):
    base = jnp.clip(jax.random.normal(jax.random.fold_in(key, 13), (SPAN, QH * HD), jnp.float32), -5.0, 5.0)
    return base.astype(jnp.bfloat16)


def draw_cache_key(key, part):
    base = jnp.clip(jax.random.normal(jax.random.fold_in(key, 31), (RESIDENT, KVH * HD), jnp.float32) * 2.5, -12.0, 12.0)
    return base.astype(jnp.bfloat16)


def draw_sample_query(key, part):
    base = jnp.clip(jax.random.normal(jax.random.fold_in(key, 33), (SAMPLES, QH * HD), jnp.float32), -5.0, 5.0)
    return base.astype(jnp.bfloat16)


def draw_owners(key, part):
    owner_count = NBLK // QBLK
    slots = owner_count * MOST_BLOCKS
    favored = jax.random.randint(jax.random.fold_in(key, 21), (), 0, owner_count)
    order = jax.random.permutation(jax.random.fold_in(key, 22), slots).astype(jnp.int32)
    slot_ids = jnp.arange(slots, dtype=jnp.int32)
    ranking = order + jnp.where(slot_ids // MOST_BLOCKS == favored, 0, slots).astype(jnp.int32)
    picked = jnp.argsort(ranking, stable=True)[:NBLK].astype(jnp.int32)
    shuffle = jax.random.permutation(jax.random.fold_in(key, 23), NBLK)
    return (picked[shuffle] // MOST_BLOCKS).astype(jnp.int32)


def block_levels(own_key, dims, pieces, least, top_value):
    level, own = 1.0, jax.random.fold_in(own_key, 6)
    for axis_at, blocks in pieces:
        heights = jnp.exp(jax.random.uniform(jax.random.fold_in(own, axis_at), (blocks,), jnp.float32, least / len(pieces), top_value / len(pieces)))
        level = level * jnp.repeat(heights, dims[axis_at] // blocks).reshape([-1 if axis == axis_at else 1 for axis in range(len(dims))])
    return level


def picks_of(rng, rows, number_of, top, lift):
    sequence = jax.random.permutation(jax.random.fold_in(rng, 1), number_of)
    favour = sequence
    for power in range(3):
        favour = favour * favour // number_of
    favour = favour * lift // number_of
    lots = jax.random.randint(jax.random.fold_in(rng, 2), (rows, number_of), 0, 4096) + favour
    sure = jax.random.permutation(jax.random.fold_in(rng, 3), rows)[jnp.arange(number_of) % rows]
    lots = jnp.where(jnp.arange(rows)[:, None] == sure[None, :], 1 << 14, lots)
    priority = lots * number_of + jnp.arange(number_of)
    return lax.top_k(priority.astype(jnp.int32), top)[1].astype(jnp.int32)


def centred(stream_key, extent, spread, limit, cuts=(), kind=jnp.bfloat16):
    factor_of = block_levels(stream_key, extent, cuts, -0.22, 0.18) if cuts else 1.0
    values = jax.random.normal(stream_key, extent, jnp.float32) * spread * factor_of
    return jnp.minimum(jnp.maximum(values, -limit), limit).astype(kind)


def setup_inputs(seed: int = 0) -> dict:
    key_of = jax.random.split(jax.random.key(seed), 12)
    span_query = draw_span_query(jax.random.fold_in(key_of[11], 71), 0)
    span_key = draw_span_key(jax.random.fold_in(key_of[11], 71), 0)
    span_value = centred(key_of[2], (SPAN, KVH * HD), 1.0, 6.0, ((0, 8), (1, 4)))
    block_lists = picks_of(key_of[3], NBLK, NBLK, KSEL, 6144)
    owners = draw_owners(jax.random.fold_in(key_of[11], 71), 0)
    cache_key = draw_cache_key(jax.random.fold_in(key_of[11], 71), 0)
    cache_value = centred(key_of[6], (RESIDENT, KVH * HD), 1.0, 6.0, ((0, 8), (1, 4)))
    sample_query = draw_sample_query(jax.random.fold_in(key_of[11], 71), 0)
    sample_key = centred(key_of[8], (SAMPLES, KVH * HD), 4.0, 24.0, ((1, 4),))
    sample_value = centred(key_of[9], (SAMPLES, KVH * HD), 1.0, 6.0, ((1, 4),))
    out_weight = centred(key_of[10], (QH * HD, D), (QH * HD) ** -0.5, 0.046875, ((0, 4), (1, 8)))
    return {"span_query": span_query, "span_key": span_key, "span_value": span_value, "block_lists": block_lists, "owners": owners, "cache_key": cache_key, "cache_value": cache_value, "sample_query": sample_query, "sample_key": sample_key, "sample_value": sample_value, "out_weight": out_weight}


NEG = -1.0e30


def reference(span_query, span_key, span_value, block_lists, owners, cache_key, cache_value, sample_query, sample_key, sample_value, out_weight):
    scale = HD ** -0.5
    group = QH // KVH
    key_blocks = span_key.reshape(NBLK, BLOCK, KVH, HD)
    value_blocks = span_value.reshape(NBLK, BLOCK, KVH, HD)
    query_blocks = span_query.reshape(NBLK, BLOCK, KVH, group, HD)
    width = (KSEL + 1) * BLOCK
    column = jnp.arange(width, dtype=jnp.int32)
    which = column // BLOCK
    within = column % BLOCK
    row_ids = jnp.arange(BLOCK, dtype=jnp.int32)

    def one_block(index):
        chosen = jnp.concatenate([index[None], block_lists[index]]).astype(jnp.int32)
        keys = key_blocks[chosen].reshape(width, KVH, HD).astype(jnp.float32)
        values = value_blocks[chosen].reshape(width, KVH, HD).astype(jnp.float32)
        queries = query_blocks[index].astype(jnp.float32)
        scores = jnp.einsum("qkgd,nkd->kgqn", queries, keys) * scale
        allowed = jnp.where(which[None, :] == 0, within[None, :] <= row_ids[:, None], (chosen[which] != index)[None, :])
        scores = jnp.where(allowed, scores, NEG)
        peak = jnp.max(scores, axis=-1, keepdims=True)
        weights = jnp.exp(scores - peak)
        probs = (weights / jnp.sum(weights, axis=-1, keepdims=True)).astype(jnp.bfloat16)
        probs = lax.optimization_barrier(probs).astype(jnp.float32)
        out = jnp.einsum("kgqn,nkd->qkgd", probs, values)
        return out.astype(jnp.bfloat16).reshape(BLOCK, QH * HD)

    span_out = lax.map(one_block, jnp.arange(NBLK, dtype=jnp.int32)).reshape(NBLK * BLOCK, QH * HD)

    owner_ids = jnp.arange(N_CTX, dtype=jnp.int32)
    mine = (owners[None, :] == owner_ids[:, None]).astype(jnp.int32)
    rank = (jnp.cumsum(mine, axis=1) - 1).astype(jnp.int32)
    slot_ids = jnp.arange(MOST_BLOCKS, dtype=jnp.int32)
    hits = (mine[:, None, :] == 1) & (rank[:, None, :] == slot_ids[None, :, None])
    picked = jnp.sum(jnp.where(hits, jnp.arange(NBLK, dtype=jnp.int32)[None, None, :], 0), axis=-1).astype(jnp.int32)
    live = jnp.any(hits, axis=-1)
    flat_keys = span_key.reshape(NBLK, BLOCK, KVH * HD)
    flat_values = span_value.reshape(NBLK, BLOCK, KVH * HD)
    appended_key = jnp.where(live[:, :, None, None], flat_keys[picked], jnp.zeros((), jnp.bfloat16)).reshape(N_CTX * MOST_BLOCKS * BLOCK, KVH * HD)
    appended_value = jnp.where(live[:, :, None, None], flat_values[picked], jnp.zeros((), jnp.bfloat16)).reshape(N_CTX * MOST_BLOCKS * BLOCK, KVH * HD)

    samples = sample_query.reshape(SAMPLES, KVH, group, HD).astype(jnp.float32)

    def group_partial(pair):
        keys, values = pair
        scores = jnp.einsum("skgd,nkd->kgsn", samples, keys.astype(jnp.float32)) * scale
        peak = jnp.max(scores, axis=-1)
        weights = jnp.exp(scores - peak[..., None])
        total = jnp.sum(weights, axis=-1)
        rounded = lax.optimization_barrier(weights.astype(jnp.bfloat16)).astype(jnp.float32)
        summed = jnp.einsum("kgsn,nkd->kgsd", rounded, values.astype(jnp.float32))
        return peak, total, summed

    res_peak, res_total, res_sum = lax.map(group_partial, (cache_key.reshape(N_CTX, RES_DEV, KVH, HD), cache_value.reshape(N_CTX, RES_DEV, KVH, HD)))
    blk_peak, blk_total, blk_sum = lax.map(group_partial, (key_blocks, value_blocks))
    peaks = jnp.concatenate([res_peak, blk_peak], axis=0)
    totals = jnp.concatenate([res_total, blk_total], axis=0)
    sums = jnp.concatenate([res_sum, blk_sum], axis=0)
    own_keys = sample_key.reshape(SAMPLES, KVH, HD).astype(jnp.float32)
    own_score = jnp.einsum("skgd,skd->kgs", samples, own_keys) * scale
    top = jnp.maximum(jnp.max(peaks, axis=0), own_score)
    factor = jnp.exp(peaks - top[None])
    own_factor = jnp.exp(own_score - top)
    total = jnp.sum(factor * totals, axis=0) + own_factor
    own_values = jnp.transpose(sample_value.reshape(SAMPLES, KVH, HD).astype(jnp.float32), (1, 0, 2))[:, None, :, :]
    combined = jnp.sum(factor[..., None] * sums, axis=0) + own_factor[..., None] * own_values
    attended = (combined / total[..., None]).astype(jnp.bfloat16)
    attended = jnp.transpose(attended, (2, 0, 1, 3)).reshape(SAMPLES, QH * HD)
    sample_out = jnp.dot(attended, out_weight, preferred_element_type=jnp.float32).astype(jnp.bfloat16)
    return span_out, sample_out, appended_key, appended_value
```

```python
import functools

import jax
import jax.numpy as jnp
from jax import lax
from jax.experimental import pallas as pl
from jax.experimental.pallas import tpu as pltpu
from jax.sharding import PartitionSpec as P

HD = 128
BLOCK = 128
MOST_BLOCKS = 8
NEG = -1e30
SCALE = HD ** -0.5
EXP2_SCALE = SCALE * 1.4426950408889634
MESH = pl.DeviceIdType.MESH
bf16, f32 = jnp.bfloat16, jnp.float32


def dot_t(a, b):
    return lax.dot_general(a, b, (((1,), (1,)), ((), ())), preferred_element_type=f32)


def dot(a, b):
    return jnp.dot(a, b, preferred_element_type=f32)


def lane_fold(op, x):
    parts = [x[:, i * 128 : (i + 1) * 128] for i in range(x.shape[1] // 128)]
    while len(parts) > 1:
        parts = [op(*parts[i : i + 2]) if i + 1 < len(parts) else parts[i] for i in range(0, len(parts), 2)]
    return parts[0]


def column(ref, head, start, size):
    return ref[pl.ds(start, size), pl.ds(pl.multiple_of(head * HD, HD), HD)]


def flip(index, mask):
    return index + mask - 2 * mask * lax.rem(lax.div(index, mask), 2)


def pack_stats(m, l, rows):
    lane = lax.broadcasted_iota(jnp.int32, (rows, 128), 1)
    both = jnp.where(lane < 4, jnp.broadcast_to(m, (rows, 128)), jnp.broadcast_to(l, (rows, 128)))
    if rows < 128:
        both = jnp.concatenate([both] * (128 // rows), axis=0)
    slabs = [both[i * 128 : (i + 1) * 128].T[:8] for i in range(max(1, rows // 128))]
    return jnp.concatenate(slabs, axis=0)


def unpack_slab(slab):
    first = lax.broadcasted_iota(jnp.int32, (8, 128), 0) < 4
    swapped = pltpu.roll(slab, 4, 0)
    return jnp.where(first, slab, swapped), jnp.where(first, swapped, slab)


def spread(slab, rows):
    return jnp.concatenate([slab] * 16, axis=0).T[: min(rows, 128)]


def merge(rows, a, b, out):
    (a_ref, a_at), (b_ref, b_at), (out_ref, out_at) = a, b, out
    first = lax.broadcasted_iota(jnp.int32, (8, 128), 0) < 4
    for i in range(max(1, rows // 128)):
        stat = slice(rows + i * 8, rows + i * 8 + 8)
        part = slice(i * 128, min((i + 1) * 128, rows))
        ma, la = unpack_slab(a_ref[(*a_at, stat, slice(None))])
        mb, lb = unpack_slab(b_ref[(*b_at, stat, slice(None))])
        top = jnp.maximum(ma, mb)
        fa = jnp.exp2((ma - top) * EXP2_SCALE)
        fb = jnp.exp2((mb - top) * EXP2_SCALE)
        acc = spread(fa, rows) * a_ref[(*a_at, part, slice(None))] + spread(fb, rows) * b_ref[(*b_at, part, slice(None))]
        out_ref[(*out_at, part, slice(None))] = acc
        out_ref[(*out_at, stat, slice(None))] = jnp.where(first, top, fa * la + fb * lb)


def decode_scores(dims, tile, q_ref, ck_ref, sk_ref, s_ref):
    samples, group, per, chunk = dims
    head = lax.div(tile * per, group)
    q = jnp.concatenate([column(q_ref, tile * per + g, 0, samples) for g in range(per)], axis=0)
    resident = ck_ref.shape[0]
    high = None
    for c in range(resident // chunk):
        s = dot_t(q, column(ck_ref, head, c * chunk, chunk))
        s_ref[:, c * chunk : (c + 1) * chunk] = s
        top = lane_fold(jnp.maximum, s)
        high = top if high is None else jnp.maximum(high, top)
    s = dot_t(q, column(sk_ref, head, 0, sk_ref.shape[0]))
    s_ref[:, resident:] = s
    peaks = [jnp.max(high, axis=1, keepdims=True)]
    for b in range(sk_ref.shape[0] // BLOCK):
        peaks.append(jnp.max(s[:, b * BLOCK : (b + 1) * BLOCK], axis=1, keepdims=True))
    return peaks


def decode_values(dims, tile, peaks, cv_ref, sv_ref, s_ref):
    samples, group, per, chunk = dims
    rows = per * samples
    head = lax.div(tile * per, group)
    resident = cv_ref.shape[0]
    total, acc = None, jnp.zeros((rows, HD), f32)
    for c in range(resident // chunk):
        w = jnp.exp2((s_ref[:, c * chunk : (c + 1) * chunk] - peaks[0]) * EXP2_SCALE)
        some = lane_fold(jnp.add, w)
        total = some if total is None else total + some
        acc = acc + dot(w.astype(bf16), column(cv_ref, head, c * chunk, chunk))
    groups = [(peaks[0], jnp.sum(total, axis=1, keepdims=True), acc)]
    for b in range(sv_ref.shape[0] // BLOCK):
        at = resident + b * BLOCK
        w = jnp.exp2((s_ref[:, at : at + BLOCK] - peaks[b + 1]) * EXP2_SCALE)
        part = dot(w.astype(bf16), column(sv_ref, head, b * BLOCK, BLOCK))
        groups.append((peaks[b + 1], jnp.sum(w, axis=1, keepdims=True), part))
    top = functools.reduce(jnp.maximum, [g[0] for g in groups])
    factors = [jnp.exp2((g[0] - top) * EXP2_SCALE) for g in groups]
    total = sum(f * g[1] for f, g in zip(factors, groups))
    acc = sum(f * g[2] for f, g in zip(factors, groups))
    return top, total, acc


def prefill_unit(dims, own, b, k, lists_ref, q_ref, kv_ref, kc_ref, vc_ref, s_refs, out_ref):
    qblk, group, ksel, heads = dims
    rows, width = heads * BLOCK, (ksel + 1) * BLOCK
    row = lax.broadcasted_iota(jnp.int32, (BLOCK, BLOCK), 0)
    col = lax.broadcasted_iota(jnp.int32, (BLOCK, BLOCK), 1)
    one_hot = jnp.where(row == col, 1.0, 0.0).astype(bf16)
    late = jnp.where(row <= col, 0.0, NEG).astype(bf16)
    for i in range(ksel + 1):
        block = own if i == 0 else lists_ref[i - 1, own]
        holder, place = lax.div(block, qblk), lax.rem(block, qblk)
        here = slice(i * BLOCK, (i + 1) * BLOCK)
        kc_ref[here, :HD] = kv_ref[holder, 0, place]
        vc_ref[here, :] = kv_ref[holder, 1, place]
        if i == 0:
            kc_ref[here, HD:] = late
        else:
            kc_ref[here, HD:] = jnp.broadcast_to(jnp.where(block == own, NEG, 0.0), (BLOCK, BLOCK)).astype(bf16)
    tiles = group // heads
    cuts = [(0, 256), (256, 256), (512, width - 512)] if width > 512 else [(0, width)]
    peaks = []
    for t in range(tiles):
        q = jnp.concatenate([column(q_ref, k * group + t * heads + g, b * BLOCK, BLOCK) for g in range(heads)], axis=0)
        q = jnp.concatenate([q, jnp.concatenate([one_hot] * heads, axis=0)], axis=1)
        high = None
        for at, size in cuts:
            s = dot_t(q, kc_ref[at : at + size, :])
            s_refs[t, :, at : at + size] = s
            top = lane_fold(jnp.maximum, s)
            high = top if high is None else jnp.maximum(high, top)
        peaks.append(jnp.max(high, axis=1, keepdims=True))
    for t in range(tiles):
        total = None
        for at, size in cuts:
            w = jnp.exp2((s_refs[t, :, at : at + size] - peaks[t]) * EXP2_SCALE)
            s_refs[t, :, at : at + size] = w
            some = lane_fold(jnp.add, w)
            total = some if total is None else total + some
        inverse = 1.0 / jnp.sum(total, axis=1, keepdims=True)
        probs = (s_refs[t, :, :] * inverse).astype(bf16)
        out = dot(probs, vc_ref[...]).astype(bf16)
        for g in range(heads):
            at = (k * group + t * heads + g) * HD
            out_ref[b * BLOCK : (b + 1) * BLOCK, at : at + HD] = out[g * BLOCK : (g + 1) * BLOCK]


def append_all(position, qblk, owners_ref, kv_refs, ak_ref, av_ref):
    blocks = owners_ref.shape[0]

    def count(b, carry):
        rank, picked = carry
        mine = owners_ref[b] == position
        picked = tuple(jnp.where(mine & (rank == slot), b, p) for slot, p in enumerate(picked))
        return rank + mine.astype(jnp.int32), picked

    rank, picked = lax.fori_loop(
        0, blocks, count, (jnp.int32(0), tuple(jnp.int32(0) for _ in range(MOST_BLOCKS)))
    )
    for slot in range(MOST_BLOCKS):
        live = jnp.broadcast_to(rank, (BLOCK, HD)) > slot
        holder, place = lax.div(picked[slot], qblk), lax.rem(picked[slot], qblk)
        for k, kv_ref in enumerate(kv_refs):
            for kind, dst in enumerate((ak_ref, av_ref)):
                x = kv_ref[holder, kind, place].astype(f32)
                dst[slot * BLOCK : (slot + 1) * BLOCK, k * HD : (k + 1) * HD] = jnp.where(live, x, 0.0).astype(bf16)


def repeat(low, high, body):
    if high - low <= 4:
        for i in range(low, high):
            body(i)
    else:

        def step(i, carry):
            body(i)
            return carry

        lax.fori_loop(low, high, step, 0)


def layer_kernel(n_ctx, n_head, dims, pre_dims, *refs):
    (lists_ref, owners_ref, q_hbm, sk_hbm, sv_hbm, ok_hbm, ov_hbm, span_k, span_v, ck_hbm, cv_hbm, sq_hbm, w_hbm) = refs[:13]
    (span_hbm, sample_ref, ak_hbm, av_hbm) = refs[13:17]
    (q_ref, sk_ref, sv_ref, ok_ref, ov_ref, ck, cv, sq, w, kv, s_ref, pre_s, kc, vc, out_v, ak, av) = refs[17:34]
    (part, below, above, cross, fresh, att, hpart, htook, hout) = refs[34:43]
    (in_sem, out_sem, g_send, g_recv, p_send, b_recv, a_recv, x_sem, t_send, t_recv, h_send, h_recv, o_send, o_recv) = refs[43:]
    samples, group, per, _ = dims
    qblk, _, ksel, _ = pre_dims
    rows = per * samples
    kvh = len(kv)
    me = lax.axis_index("ctx")
    hme = lax.axis_index("head")
    n = n_ctx // 2
    z, x = lax.div(me, 2), lax.rem(me, 2)
    pair = z * 2 + 1 - x
    bits = [1 << i for i in range(n_head.bit_length() - 1)]

    def local(index, src, dst):
        return pltpu.make_async_copy(src, dst, in_sem.at[index])

    loads = [
        local(i, a, b)
        for i, (a, b) in enumerate(
            (
                (q_hbm, q_ref),
                (ck_hbm, ck),
                (cv_hbm, cv),
                (sk_hbm, sk_ref),
                (sv_hbm, sv_ref),
                (ok_hbm, ok_ref),
                (ov_hbm, ov_ref),
                (sq_hbm, sq),
                (w_hbm, w),
            )
        )
    ]
    mine = [
        local(9 + p * 2 + kind, src.at[:, :, pl.ds(p * HD, HD)], kv[p].at[me, kind])
        for p in range(kvh)
        for kind, src in enumerate((span_k, span_v))
    ]
    for copy in mine + loads[:7]:
        copy.start()

    barrier = pltpu.get_barrier_semaphore()
    for j in range(1, n):
        pl.semaphore_signal(barrier, inc=1, device_id={"ctx": lax.rem(z + j, n) * 2 + x}, device_id_type=MESH)
    pl.semaphore_signal(barrier, inc=1, device_id={"ctx": pair}, device_id_type=MESH)
    for bit in bits:
        pl.semaphore_signal(barrier, inc=1, device_id={"head": flip(hme, bit)}, device_id_type=MESH)
    pl.semaphore_wait(barrier, n + len(bits))
    for copy in mine:
        copy.wait()

    def send(src, dst, ssem, rsem, axis, to):
        return pltpu.make_async_remote_copy(
            src_ref=src, dst_ref=dst, send_sem=ssem, recv_sem=rsem, device_id={axis: to}, device_id_type=MESH
        )

    class Line:
        def __init__(self, buf, ssem, rsem):
            self.buf, self.ssem, self.rsem = buf, ssem, rsem

        def copy(self, owner, way, to):
            view = self.buf.at[owner]
            return send(view, view, self.ssem.at[way, owner], self.rsem.at[owner], "ctx", to)

        def each(self, s, act):
            if isinstance(s, int) and s == 0:
                act(self.copy(me, 0, pair))
                pl.when(z + 1 < n)(lambda: act(self.copy(me, 1, me + 2)))
                pl.when(z > 0)(lambda: act(self.copy(me, 2, me - 2)))
                return

            def up():
                act(self.copy(me - 2 * s, 0, pair))
                pl.when(z + 1 < n)(lambda: act(self.copy(me - 2 * s, 1, me + 2)))

            def down():
                act(self.copy(me + 2 * s, 0, pair))
                pl.when(z > 0)(lambda: act(self.copy(me + 2 * s, 2, me - 2)))

            pl.when(z - s >= 0)(up)
            pl.when(z + s < n)(down)

        def start(self):
            self.each(0, lambda c: c.start())

        def landed(self, owner):
            self.copy(owner, 0, pair).wait_recv()

        def forward(self, s):
            pl.when(z - s >= 0)(lambda: self.landed(me - 2 * s))
            pl.when(z + s < n)(lambda: self.landed(me + 2 * s))
            self.each(s, lambda c: c.start())

        def finish(self):
            repeat(0, n, lambda j: self.landed(j * 2 + 1 - x))

        def drain(self):
            self.each(0, lambda c: c.wait_send())
            repeat(1, n, lambda s: self.each(s, lambda c: c.wait_send()))

    gathers = [Line(kv[p], g_send[p], g_recv[p]) for p in range(kvh)]
    gathers[0].start()

    for i in (0, 5, 6):
        loads[i].wait()
    key_head = lax.div(me * per, group)
    own_key = column(ok_ref, key_head, 0, samples).astype(f32)
    own = [
        jnp.sum(column(q_ref, me * per + g, 0, samples).astype(f32) * own_key, axis=1, keepdims=True)
        for g in range(per)
    ]
    fresh[:rows, :] = jnp.concatenate([column(ov_ref, key_head, 0, samples).astype(f32)] * per, axis=0)
    fresh[rows:, :] = pack_stats(jnp.concatenate(own, axis=0), jnp.ones((rows, 1), f32), rows)
    for i in (1, 2, 3, 4):
        loads[i].wait()
    loads[7].start()
    loads[8].start()

    def up_copy(d, t, rsem=b_recv, dst=below):
        return send(part.at[d, t], dst.at[d, t], p_send.at[d, t], rsem.at[d, t], "ctx", me + 2)

    def down_copy(d, t, rsem=a_recv, dst=above):
        return send(part.at[d, t], dst.at[d, t], p_send.at[d, t], rsem.at[d, t], "ctx", me - 2)

    way = 2 * lax.div(z, n // 2) - 1

    def decode_step(i, carry):
        d = lax.rem(z + way * (1 + i) + 2 * n, n)
        peaks = [decode_scores(dims, d * 2 + t, q_ref, ck, sk_ref, s_ref.at[t]) for t in range(2)]
        for t in range(2):
            m, l, acc = decode_values(dims, d * 2 + t, peaks[t], cv, sv_ref, s_ref.at[t])
            part[d, t, :rows, :] = acc
            part[d, t, rows:, :] = pack_stats(m, l, rows)

        @pl.when((z == 0) & (i < n - 1))
        def _():
            for t in range(2):
                up_copy(d, t).start()

        @pl.when((z == n - 1) & (i < n - 1))
        def _():
            for t in range(2):
                down_copy(d, t).start()

        @pl.when(i < n - 1)
        def _():
            gathers[0].forward(i + 1)

        @pl.when(i == 0)
        def _():
            for g in gathers[1:]:
                g.start()

        @pl.when(i >= 2)
        def _():
            for g in gathers[1:]:
                g.forward(i - 1)

        return carry

    lax.fori_loop(0, n, decode_step, 0)

    def collect(e):
        def from_below():
            for t in range(2):
                d = n - 1 - e
                down_copy(d, t, b_recv, below).wait_recv()
                merge(rows, (part, (d, t)), (below, (d, t)), (part, (d, t)))
                pl.when(d > z)(lambda: up_copy(d, t).start())

        def from_above():
            for t in range(2):
                d = e
                up_copy(d, t, a_recv, above).wait_recv()
                merge(rows, (part, (d, t)), (above, (d, t)), (part, (d, t)))
                pl.when(d < z)(lambda: down_copy(d, t).start())

        pl.when((z > 0) & (n - 1 - e >= z))(from_below)
        pl.when((z < n - 1) & (e <= z))(from_above)

    def prefill(b, p):
        prefill_unit(pre_dims, me * qblk + b, b, p, lists_ref, sq, kv[p], kc, vc, pre_s, out_v)
        if p == kvh - 1:
            span_copy(b).start()

    def span_copy(b):
        where = pl.ds(b * BLOCK, BLOCK)
        return pltpu.make_async_copy(out_v.at[where], span_hbm.at[where], out_sem.at[b])

    slots = [
        pltpu.make_async_copy(ak, ak_hbm, out_sem.at[qblk]),
        pltpu.make_async_copy(av, av_hbm, out_sem.at[qblk + 1]),
    ]

    cross_copy = send(part.at[z, 1 - x], cross, x_sem.at[0], x_sem.at[1], "ctx", pair)

    def attended():
        merge(rows, (part, (z, x)), (fresh, ()), (fresh, ()))
        cross_copy.wait_recv()
        merge(rows, (fresh, ()), (cross, ()), (fresh, ()))
        for i in range(max(1, rows // 128)):
            size = min(rows, 128)
            _, l = unpack_slab(fresh[rows + i * 8 : rows + i * 8 + 8, :])
            done = (fresh[i * 128 : i * 128 + size, :] * spread(1.0 / l, rows)).astype(bf16)
            for g in range(size // samples):
                head = i * (128 // samples) + g
                att[me, :, head * HD : (head + 1) * HD] = done[g * samples : (g + 1) * samples]

    columns = w.shape[1] // n_head
    depth = per * HD

    def att_copy(index, owner, to):
        view = att.at[owner]
        return send(view, view, t_send.at[index], t_recv.at[owner], "ctx", to)

    def line_at(j):
        return lax.rem(z - j + n, n) * 2

    def att_start():
        att_copy(0, me, pair).start()
        for j in range(1, n):
            att_copy(j, me, lax.rem(z + j, n) * 2 + x).start()

    def head_copies(index):
        bit = bits[index]
        return [
            (j, send(hpart.at[j], htook.at[j], h_send.at[j], h_recv.at[j], "head", flip(hme, bit)))
            for j in range(bit, n_head, 2 * bit)
        ]

    def terms(owner, first=False, last=False):
        order = sorted(range(n_head), key=lambda j: [1 - (j & bit) // bit for bit in bits])
        starts = dict(head_copies(0)) if last else {}
        for j in order:
            chunk = hme
            for bit in bits:
                if j & bit:
                    chunk = flip(chunk, bit)
            where = pl.ds(pl.multiple_of(chunk * columns, 128), columns)
            x = dot(att[owner], w[pl.ds(pl.multiple_of(owner * depth, 128), depth), where])
            hpart[j] = x if first else hpart[j] + x
            if j in starts:
                starts[j].start()

    def project():
        loads[8].wait()
        terms(me, first=True)

        def straight(j):
            owner = line_at(j) + x
            att_copy(0, owner, pair).wait_recv()
            att_copy(n - 1 + j, owner, pair).start()
            terms(owner)

        def paired(j):
            owner = line_at(j) + 1 - x
            att_copy(0, owner, pair).wait_recv()
            terms(owner)

        repeat(1, n, straight)
        repeat(0, n - 1, paired)
        owner = line_at(n - 1) + 1 - x
        att_copy(0, owner, pair).wait_recv()
        terms(owner, last=True)

    def halve(index):
        if index:
            for _, copy in head_copies(index):
                copy.start()
        for j, copy in head_copies(index):
            copy.wait_recv()
            hpart[j - bits[index]] = hpart[j - bits[index]] + htook[j]

    def out_copies(index):
        bit = bits[index]
        return [
            send(hout.at[j], hout.at[j + bit], o_send.at[j + bit], o_recv.at[j + bit], "head", flip(hme, bit))
            for j in range(0, n_head, 2 * bit)
        ]

    gathers[0].finish()
    loads[7].wait()
    prefill(0, 0)
    collect(0)
    for g in gathers[1:]:
        g.forward(n - 1)
    for b in range(1, qblk):
        prefill(b, 0)
    repeat(1, n, collect)
    cross_copy.start()
    for g in gathers[1:]:
        g.finish()
    append_all(me, qblk, owners_ref, kv, ak, av)
    for copy in slots:
        copy.start()
    attended()
    att_start()
    rest = [(b, p) for p in range(1, kvh) for b in range(qblk)]
    for b, p in rest[: len(rest) // 2]:
        prefill(b, p)
    project()
    for b, p in rest[len(rest) // 2 :]:
        prefill(b, p)
    for index in range(len(bits)):
        halve(index)
    hout[0] = hpart[0].astype(bf16)
    for index in reversed(range(len(bits))):
        for copy in out_copies(index):
            copy.start()
        for copy in out_copies(index):
            copy.wait_recv()
    for j in range(n_head):
        chunk = hme
        for bit in bits:
            if j & bit:
                chunk = flip(chunk, bit)
        sample_ref[:, pl.ds(pl.multiple_of(chunk * columns, 128), columns)] = hout[j]

    for g in gathers:
        g.drain()
    for t in range(2):

        def sent(d, t=t):
            pl.when(d != z)(lambda: send(part.at[d, t], below.at[d, t], p_send.at[d, t], b_recv.at[d, t], "ctx", pair).wait_send())

        repeat(0, n, sent)
    cross_copy.wait_send()
    for j in range(n):
        att_copy(j, me, pair).wait_send()
    for j in range(1, n):
        att_copy(n - 1 + j, line_at(j) + x, pair).wait_send()
    for index in range(len(bits)):
        for _, copy in head_copies(index):
            copy.wait_send()
        for copy in out_copies(index):
            copy.wait_send()
    for b in range(qblk):
        span_copy(b).wait()
    for copy in slots:
        copy.wait()


VM = pl.BlockSpec(memory_space=pltpu.VMEM)
SM = pl.BlockSpec(memory_space=pltpu.SMEM)
ANY = pl.BlockSpec(memory_space=pl.ANY)


def local(n_ctx, n_head, span_query, span_key, span_value, block_lists, owners, cache_key, cache_value, sample_query, sample_key, sample_value, out_weight):
    tokens = span_query.shape[0]
    kvh = span_key.shape[1] // HD
    group = span_query.shape[1] // HD // kvh
    qblk = tokens // BLOCK
    samples = sample_query.shape[0]
    per = kvh * group // n_ctx
    rows = per * samples
    resident = cache_key.shape[0]
    ksel = block_lists.shape[1]
    width = (ksel + 1) * BLOCK
    wide = kvh * HD
    columns = out_weight.shape[1] // n_head
    packet = rows + 8 * max(1, rows // 128)
    heads = 4
    n = n_ctx // 2
    slots = jax.ShapeDtypeStruct((MOST_BLOCKS * BLOCK, wide), bf16)
    dma = pltpu.SemaphoreType.DMA
    vm = pltpu.VMEM
    return pl.pallas_call(
        functools.partial(layer_kernel, n_ctx, n_head, (samples, group, per, 512), (qblk, group, ksel, heads)),
        out_shape=(
            jax.ShapeDtypeStruct(span_query.shape, bf16),
            jax.ShapeDtypeStruct((samples, out_weight.shape[1]), bf16),
            slots,
            slots,
        ),
        in_specs=[SM, SM] + [ANY] * 11,
        out_specs=(ANY, VM, ANY, ANY),
        scratch_shapes=[
            vm(sample_query.shape, bf16),
            vm(span_key.shape, bf16),
            vm(span_value.shape, bf16),
            vm(sample_key.shape, bf16),
            vm(sample_value.shape, bf16),
            vm(cache_key.shape, bf16),
            vm(cache_value.shape, bf16),
            vm(span_query.shape, bf16),
            vm(out_weight.shape, bf16),
            [vm((n_ctx, 2, qblk, BLOCK, HD), bf16) for _ in range(kvh)],
            vm((2, rows, resident + tokens), f32),
            vm((group // heads, heads * BLOCK, width), f32),
            vm((width, 2 * HD), bf16),
            vm((width, HD), bf16),
            vm(span_query.shape, bf16),
            vm(slots.shape, bf16),
            vm(slots.shape, bf16),
            vm((n, 2, packet, HD), f32),
            vm((n, 2, packet, HD), f32),
            vm((n, 2, packet, HD), f32),
            vm((packet, HD), f32),
            vm((packet, HD), f32),
            vm((n_ctx, samples, per * HD), bf16),
            vm((n_head, samples, columns), f32),
            vm((n_head, samples, columns), f32),
            vm((n_head, samples, columns), bf16),
            dma((9 + 2 * kvh,)),
            dma((qblk + 2,)),
            [dma((3, n_ctx)) for _ in range(kvh)],
            [dma((n_ctx,)) for _ in range(kvh)],
            dma((n, 2)),
            dma((n, 2)),
            dma((n, 2)),
            dma((2,)),
            dma((2 * n,)),
            dma((n_ctx,)),
            dma((n_head,)),
            dma((n_head,)),
            dma((n_head,)),
            dma((n_head,)),
        ],
        compiler_params=pltpu.CompilerParams(
            vmem_limit_bytes=60 << 20, collective_id=0, has_side_effects=True
        ),
        name="layer",
    )(
        block_lists.T,
        owners,
        sample_query,
        span_key,
        span_value,
        sample_key,
        sample_value,
        span_key.reshape(qblk, BLOCK, wide),
        span_value.reshape(qblk, BLOCK, wide),
        cache_key,
        cache_value,
        span_query,
        out_weight,
    )


def solution(mesh):
    c = P("ctx", "head")
    return jax.shard_map(
        functools.partial(local, mesh.shape["ctx"], mesh.shape["head"]),
        mesh=mesh,
        in_specs=(c, c, c, P(), P(), c, c, P(None, "head"), P(None, "head"), P(None, "head"), P("head", "ctx")),
        out_specs=(c, P(None, "ctx"), c, c),
        check_vma=False,
    )
```

```python
import functools

import jax
import jax.numpy as jnp
from jax import lax
from jax.experimental import pallas as pl
from jax.experimental.pallas import tpu as pltpu
from jax.sharding import PartitionSpec as P

HD = 128
BLOCK = 128
MOST_BLOCKS = 8
NEG = -1e30
SCALE = HD ** -0.5
EXP2_SCALE = SCALE * 1.4426950408889634
MESH = pl.DeviceIdType.MESH
bf16, f32 = jnp.bfloat16, jnp.float32


def dot_t(a, b):
    return lax.dot_general(a, b, (((1,), (1,)), ((), ())), preferred_element_type=f32)


def dot(a, b):
    return jnp.dot(a, b, preferred_element_type=f32)


def lane_fold(op, x):
    parts = [x[:, i * 128 : (i + 1) * 128] for i in range(x.shape[1] // 128)]
    while len(parts) > 1:
        parts = [op(*parts[i : i + 2]) if i + 1 < len(parts) else parts[i] for i in range(0, len(parts), 2)]
    return parts[0]


def column(ref, head, start, size):
    return ref[pl.ds(start, size), pl.ds(pl.multiple_of(head * HD, HD), HD)]


def flip(index, mask):
    return index + mask - 2 * mask * lax.rem(lax.div(index, mask), 2)


def pack_stats(m, l, rows):
    lane = lax.broadcasted_iota(jnp.int32, (rows, 128), 1)
    both = jnp.where(lane < 4, jnp.broadcast_to(m, (rows, 128)), jnp.broadcast_to(l, (rows, 128)))
    if rows < 128:
        both = jnp.concatenate([both] * (128 // rows), axis=0)
    slabs = [both[i * 128 : (i + 1) * 128].T[:8] for i in range(max(1, rows // 128))]
    return jnp.concatenate(slabs, axis=0)


def unpack_slab(slab):
    first = lax.broadcasted_iota(jnp.int32, (8, 128), 0) < 4
    swapped = pltpu.roll(slab, 4, 0)
    return jnp.where(first, slab, swapped), jnp.where(first, swapped, slab)


def spread(slab, rows):
    return jnp.concatenate([slab] * 16, axis=0).T[: min(rows, 128)]


def merge(rows, a, b, out):
    (a_ref, a_at), (b_ref, b_at), (out_ref, out_at) = a, b, out
    first = lax.broadcasted_iota(jnp.int32, (8, 128), 0) < 4
    for i in range(max(1, rows // 128)):
        stat = slice(rows + i * 8, rows + i * 8 + 8)
        part = slice(i * 128, min((i + 1) * 128, rows))
        ma, la = unpack_slab(a_ref[(*a_at, stat, slice(None))])
        mb, lb = unpack_slab(b_ref[(*b_at, stat, slice(None))])
        top = jnp.maximum(ma, mb)
        fa = jnp.exp2((ma - top) * EXP2_SCALE)
        fb = jnp.exp2((mb - top) * EXP2_SCALE)
        acc = spread(fa, rows) * a_ref[(*a_at, part, slice(None))] + spread(fb, rows) * b_ref[(*b_at, part, slice(None))]
        out_ref[(*out_at, part, slice(None))] = acc
        out_ref[(*out_at, stat, slice(None))] = jnp.where(first, top, fa * la + fb * lb)


def decode_scores(dims, tile, q_ref, ck_ref, sk_ref, s_ref):
    samples, group, per, chunk = dims
    head = lax.div(tile * per, group)
    q = jnp.concatenate([column(q_ref, tile * per + g, 0, samples) for g in range(per)], axis=0)
    resident = ck_ref.shape[0]
    high = None
    for c in range(resident // chunk):
        s = dot_t(q, column(ck_ref, head, c * chunk, chunk))
        s_ref[:, c * chunk : (c + 1) * chunk] = s
        top = lane_fold(jnp.maximum, s)
        high = top if high is None else jnp.maximum(high, top)
    s = dot_t(q, column(sk_ref, head, 0, sk_ref.shape[0]))
    s_ref[:, resident:] = s
    peaks = [jnp.max(high, axis=1, keepdims=True)]
    for b in range(sk_ref.shape[0] // BLOCK):
        peaks.append(jnp.max(s[:, b * BLOCK : (b + 1) * BLOCK], axis=1, keepdims=True))
    return peaks


def decode_values(dims, tile, peaks, cv_ref, sv_ref, s_ref):
    samples, group, per, chunk = dims
    rows = per * samples
    head = lax.div(tile * per, group)
    resident = cv_ref.shape[0]
    total, acc = None, jnp.zeros((rows, HD), f32)
    for c in range(resident // chunk):
        w = jnp.exp2((s_ref[:, c * chunk : (c + 1) * chunk] - peaks[0]) * EXP2_SCALE)
        some = lane_fold(jnp.add, w)
        total = some if total is None else total + some
        acc = acc + dot(w.astype(bf16), column(cv_ref, head, c * chunk, chunk))
    groups = [(peaks[0], jnp.sum(total, axis=1, keepdims=True), acc)]
    for b in range(sv_ref.shape[0] // BLOCK):
        at = resident + b * BLOCK
        w = jnp.exp2((s_ref[:, at : at + BLOCK] - peaks[b + 1]) * EXP2_SCALE)
        part = dot(w.astype(bf16), column(sv_ref, head, b * BLOCK, BLOCK))
        groups.append((peaks[b + 1], jnp.sum(w, axis=1, keepdims=True), part))
    top = functools.reduce(jnp.maximum, [g[0] for g in groups])
    factors = [jnp.exp2((g[0] - top) * EXP2_SCALE) for g in groups]
    total = sum(f * g[1] for f, g in zip(factors, groups))
    acc = sum(f * g[2] for f, g in zip(factors, groups))
    return top, total, acc


def prefill_unit(dims, own, b, k, lists_ref, q_ref, kv_ref, kc_ref, vc_ref, s_refs, out_ref):
    qblk, group, ksel, heads = dims
    rows, width = heads * BLOCK, (ksel + 1) * BLOCK
    row = lax.broadcasted_iota(jnp.int32, (BLOCK, BLOCK), 0)
    col = lax.broadcasted_iota(jnp.int32, (BLOCK, BLOCK), 1)
    one_hot = jnp.where(row == col, 1.0, 0.0).astype(bf16)
    late = jnp.where(row <= col, 0.0, NEG).astype(bf16)
    for i in range(ksel + 1):
        block = own if i == 0 else lists_ref[i - 1, own]
        holder, place = lax.div(block, qblk), lax.rem(block, qblk)
        here = slice(i * BLOCK, (i + 1) * BLOCK)
        kc_ref[here, :HD] = kv_ref[holder, 0, place]
        vc_ref[here, :] = kv_ref[holder, 1, place]
        if i == 0:
            kc_ref[here, HD:] = late
        else:
            kc_ref[here, HD:] = jnp.broadcast_to(jnp.where(block == own, NEG, 0.0), (BLOCK, BLOCK)).astype(bf16)
    tiles = group // heads
    cuts = [(0, 256), (256, 256), (512, width - 512)] if width > 512 else [(0, width)]
    peaks = []
    for t in range(tiles):
        q = jnp.concatenate([column(q_ref, k * group + t * heads + g, b * BLOCK, BLOCK) for g in range(heads)], axis=0)
        q = jnp.concatenate([q, jnp.concatenate([one_hot] * heads, axis=0)], axis=1)
        high = None
        for at, size in cuts:
            s = dot_t(q, kc_ref[at : at + size, :])
            s_refs[t, :, at : at + size] = s
            top = lane_fold(jnp.maximum, s)
            high = top if high is None else jnp.maximum(high, top)
        peaks.append(jnp.max(high, axis=1, keepdims=True))
    for t in range(tiles):
        total = None
        for at, size in cuts:
            w = jnp.exp2((s_refs[t, :, at : at + size] - peaks[t]) * EXP2_SCALE)
            s_refs[t, :, at : at + size] = w
            some = lane_fold(jnp.add, w)
            total = some if total is None else total + some
        inverse = 1.0 / jnp.sum(total, axis=1, keepdims=True)
        probs = (s_refs[t, :, :] * inverse).astype(bf16)
        out = dot(probs, vc_ref[...]).astype(bf16)
        for g in range(heads):
            at = (k * group + t * heads + g) * HD
            out_ref[b * BLOCK : (b + 1) * BLOCK, at : at + HD] = out[g * BLOCK : (g + 1) * BLOCK]


def append_all(position, qblk, owners_ref, kv_refs, ak_ref, av_ref):
    blocks = owners_ref.shape[0]

    def count(b, carry):
        rank, picked = carry
        mine = owners_ref[b] == position
        picked = tuple(jnp.where(mine & (rank == slot), b, p) for slot, p in enumerate(picked))
        return rank + mine.astype(jnp.int32), picked

    rank, picked = lax.fori_loop(
        0, blocks, count, (jnp.int32(0), tuple(jnp.int32(0) for _ in range(MOST_BLOCKS)))
    )
    for slot in range(MOST_BLOCKS):
        live = jnp.broadcast_to(rank, (BLOCK, HD)) > slot
        holder, place = lax.div(picked[slot], qblk), lax.rem(picked[slot], qblk)
        for k, kv_ref in enumerate(kv_refs):
            for kind, dst in enumerate((ak_ref, av_ref)):
                x = kv_ref[holder, kind, place].astype(f32)
                dst[slot * BLOCK : (slot + 1) * BLOCK, k * HD : (k + 1) * HD] = jnp.where(live, x, 0.0).astype(bf16)


def repeat(low, high, body):
    if high - low <= 4:
        for i in range(low, high):
            body(i)
    else:

        def step(i, carry):
            body(i)
            return carry

        lax.fori_loop(low, high, step, 0)


def layer_kernel(n_ctx, n_head, dims, pre_dims, *refs):
    (lists_ref, owners_ref, q_hbm, sk_hbm, sv_hbm, ok_hbm, ov_hbm, span_k, span_v, ck_hbm, cv_hbm, sq_hbm, w_hbm) = refs[:13]
    (span_hbm, sample_ref, ak_hbm, av_hbm) = refs[13:17]
    (q_ref, sk_ref, sv_ref, ok_ref, ov_ref, ck, cv, sq, w, kv, s_ref, pre_s, kc, vc, out_v, ak, av) = refs[17:34]
    (part, below, above, cross, fresh, att, hpart, htook, hout) = refs[34:43]
    (in_sem, out_sem, g_send, g_recv, p_send, b_recv, a_recv, c_send, c_recv, t_send, t_recv, h_send, h_recv, o_send, o_recv) = refs[43:]
    samples, group, per, _ = dims
    qblk, _, ksel, _ = pre_dims
    rows = per * samples
    kvh = len(kv)
    me = lax.axis_index("ctx")
    hme = lax.axis_index("head")
    n = n_ctx // 2
    z, x = lax.div(me, 2), lax.rem(me, 2)
    pair = z * 2 + 1 - x
    bits = [1 << i for i in range(n_head.bit_length() - 1)]

    def local(index, src, dst):
        return pltpu.make_async_copy(src, dst, in_sem.at[index])

    loads = [
        local(i, a, b)
        for i, (a, b) in enumerate(
            (
                (q_hbm, q_ref),
                (ck_hbm, ck),
                (cv_hbm, cv),
                (sk_hbm, sk_ref),
                (sv_hbm, sv_ref),
                (ok_hbm, ok_ref),
                (ov_hbm, ov_ref),
                (sq_hbm, sq),
                (w_hbm, w),
            )
        )
    ]
    mine = [
        local(9 + p * 2 + kind, src.at[:, :, pl.ds(p * HD, HD)], kv[p].at[me, kind])
        for p in range(kvh)
        for kind, src in enumerate((span_k, span_v))
    ]
    for copy in mine + loads[:7]:
        copy.start()

    barrier = pltpu.get_barrier_semaphore()
    for j in range(1, n):
        pl.semaphore_signal(barrier, inc=1, device_id={"ctx": lax.rem(z + j, n) * 2 + x}, device_id_type=MESH)
    pl.semaphore_signal(barrier, inc=1, device_id={"ctx": pair}, device_id_type=MESH)
    for bit in bits:
        pl.semaphore_signal(barrier, inc=1, device_id={"head": flip(hme, bit)}, device_id_type=MESH)
    pl.semaphore_wait(barrier, n + len(bits))
    for copy in mine:
        copy.wait()

    def send(src, dst, ssem, rsem, axis, to):
        return pltpu.make_async_remote_copy(
            src_ref=src, dst_ref=dst, send_sem=ssem, recv_sem=rsem, device_id={axis: to}, device_id_type=MESH
        )

    class Line:
        def __init__(self, buf, ssem, rsem, pair_first):
            self.buf, self.ssem, self.rsem, self.pair_first = buf, ssem, rsem, pair_first

        def copy(self, owner, way, to):
            view = self.buf.at[owner]
            return send(view, view, self.ssem.at[way, owner], self.rsem.at[owner], "ctx", to)

        def landed(self, owner):
            self.copy(owner, 0, pair).wait_recv()

        def up(self, owner, act):
            pl.when(z + 1 < n)(lambda: act(self.copy(owner, 1, me + 2)))

        def down(self, owner, act):
            pl.when(z > 0)(lambda: act(self.copy(owner, 2, me - 2)))

        def own(self, act):
            act(self.copy(me, 0, pair))
            self.up(me, act)
            self.down(me, act)

        def paired(self, act):
            if self.pair_first:
                self.up(pair, act)
                self.down(pair, act)

        def hops(self, base, s, act):
            def from_below():
                if not self.pair_first:
                    act(self.copy(base - 2 * s, 0, pair))
                self.up(base - 2 * s, act)

            def from_above():
                if not self.pair_first:
                    act(self.copy(base + 2 * s, 0, pair))
                self.down(base + 2 * s, act)

            pl.when(z - s >= 0)(from_below)
            pl.when(z + s < n)(from_above)

        def start(self):
            self.own(lambda c: c.start())

        def forward_pair(self):
            self.landed(pair)
            self.paired(lambda c: c.start())

        def forward(self, base, s):
            pl.when(z - s >= 0)(lambda: self.landed(base - 2 * s))
            pl.when(z + s < n)(lambda: self.landed(base + 2 * s))
            self.hops(base, s, lambda c: c.start())

        def finish(self):
            repeat(0, n, lambda j: self.landed(j * 2 + 1 - x))

        def drain(self):
            def done(c):
                c.wait_send()

            self.own(done)
            self.paired(done)
            for base in (me, pair) if self.pair_first else (me,):
                repeat(1, n, lambda s: self.hops(base, s, done))

    gathers = [Line(kv[p], g_send[p], g_recv[p], p == 0) for p in range(kvh)]
    gathers[0].start()

    for i in (0, 5, 6):
        loads[i].wait()
    key_head = lax.div(me * per, group)
    own_key = column(ok_ref, key_head, 0, samples).astype(f32)
    own = [
        jnp.sum(column(q_ref, me * per + g, 0, samples).astype(f32) * own_key, axis=1, keepdims=True)
        for g in range(per)
    ]
    fresh[:rows, :] = jnp.concatenate([column(ov_ref, key_head, 0, samples).astype(f32)] * per, axis=0)
    fresh[rows:, :] = pack_stats(jnp.concatenate(own, axis=0), jnp.ones((rows, 1), f32), rows)
    for i in (1, 2, 3, 4):
        loads[i].wait()
    loads[7].start()
    loads[8].start()

    def cross_copy(d):
        return send(part.at[d, 1 - x], cross.at[d], c_send.at[d], c_recv.at[d], "ctx", pair)

    def up_copy(d):
        return send(part.at[d, x], below.at[d], p_send.at[d], b_recv.at[d], "ctx", me + 2)

    def down_copy(d):
        return send(part.at[d, x], above.at[d], p_send.at[d], a_recv.at[d], "ctx", me - 2)

    way = 2 * lax.div(z, n // 2) - 1

    def unit_at(i):
        return lax.rem(z + way * (1 + i) + 2 * n, n)

    def take_cross(d):
        cross_copy(d).wait_recv()
        merge(rows, (part, (d, x)), (cross, (d,)), (part, (d, x)))

    def collect(r):
        def from_below():
            d = n - 1 - r + z
            send(part.at[d, x], below.at[d], p_send.at[d], b_recv.at[d], "ctx", pair).wait_recv()
            merge(rows, (part, (d, x)), (below, (d,)), (part, (d, x)))
            pl.when(d > z)(lambda: up_copy(d).start())

        def from_above():
            d = r - (n - 1) + z
            send(part.at[d, x], above.at[d], p_send.at[d], a_recv.at[d], "ctx", pair).wait_recv()
            merge(rows, (part, (d, x)), (above, (d,)), (part, (d, x)))
            pl.when(d < z)(lambda: down_copy(d).start())

        pl.when((z > 0) & (r >= z))(from_below)
        pl.when((z < n - 1) & (r + z >= n - 1))(from_above)

    def decode_step(i, carry):
        d = unit_at(i)
        peaks = [decode_scores(dims, d * 2 + t, q_ref, ck, sk_ref, s_ref.at[t]) for t in range(2)]
        for t in range(2):
            m, l, acc = decode_values(dims, d * 2 + t, peaks[t], cv, sv_ref, s_ref.at[t])
            part[d, t, :rows, :] = acc
            part[d, t, rows:, :] = pack_stats(m, l, rows)
        cross_copy(d).start()

        @pl.when(i >= 1)
        def _():
            before = unit_at(i - 1)
            take_cross(before)
            pl.when(z == 0)(lambda: up_copy(before).start())
            pl.when(z == n - 1)(lambda: down_copy(before).start())

        @pl.when(i == 0)
        def _():
            gathers[0].forward_pair()

        @pl.when((i >= 1) & (i < n - 1))
        def _():
            gathers[0].forward(pair, i)

        @pl.when(i < n - 1)
        def _():
            gathers[0].forward(me, i + 1)

        @pl.when(i == n - 2)
        def _():
            for g in gathers[1:]:
                g.start()
            collect(1)

        return carry

    lax.fori_loop(0, n, decode_step, 0)

    def prefill(b, p):
        prefill_unit(pre_dims, me * qblk + b, b, p, lists_ref, sq, kv[p], kc, vc, pre_s, out_v)
        if p == kvh - 1:
            span_copy(b).start()

    def span_copy(b):
        where = pl.ds(b * BLOCK, BLOCK)
        return pltpu.make_async_copy(out_v.at[where], span_hbm.at[where], out_sem.at[b])

    slots = [
        pltpu.make_async_copy(ak, ak_hbm, out_sem.at[qblk]),
        pltpu.make_async_copy(av, av_hbm, out_sem.at[qblk + 1]),
    ]

    def attended():
        merge(rows, (part, (z, x)), (fresh, ()), (fresh, ()))
        for i in range(max(1, rows // 128)):
            size = min(rows, 128)
            _, l = unpack_slab(fresh[rows + i * 8 : rows + i * 8 + 8, :])
            done = (fresh[i * 128 : i * 128 + size, :] * spread(1.0 / l, rows)).astype(bf16)
            for g in range(size // samples):
                head = i * (128 // samples) + g
                att[me, :, head * HD : (head + 1) * HD] = done[g * samples : (g + 1) * samples]

    columns = w.shape[1] // n_head
    depth = per * HD

    def att_copy(index, owner, to):
        view = att.at[owner]
        return send(view, view, t_send.at[index], t_recv.at[owner], "ctx", to)

    def line_at(j):
        return lax.rem(z - j + n, n) * 2

    def att_start():
        att_copy(0, me, pair).start()
        for j in range(1, n):
            att_copy(j, me, lax.rem(z + j, n) * 2 + x).start()

    def head_copies(index):
        bit = bits[index]
        return [
            (j, send(hpart.at[j], htook.at[j], h_send.at[j], h_recv.at[j], "head", flip(hme, bit)))
            for j in range(bit, n_head, 2 * bit)
        ]

    def terms(owner, first=False, last=False):
        order = sorted(range(n_head), key=lambda j: [1 - (j & bit) // bit for bit in bits])
        starts = dict(head_copies(0)) if last else {}
        for j in order:
            chunk = hme
            for bit in bits:
                if j & bit:
                    chunk = flip(chunk, bit)
            where = pl.ds(pl.multiple_of(chunk * columns, 128), columns)
            x = dot(att[owner], w[pl.ds(pl.multiple_of(owner * depth, 128), depth), where])
            hpart[j] = x if first else hpart[j] + x
            if j in starts:
                starts[j].start()

    def att_forward(j):
        owner = line_at(j) + x
        att_copy(0, owner, pair).wait_recv()
        att_copy(n - 1 + j, owner, pair).start()

    def project():
        loads[8].wait()
        terms(me, first=True)

        def straight(j):
            terms(line_at(j) + x)

        def paired(j):
            owner = line_at(j) + 1 - x
            att_copy(0, owner, pair).wait_recv()
            terms(owner)

        repeat(1, n, straight)
        repeat(0, n - 1, paired)
        owner = line_at(n - 1) + 1 - x
        att_copy(0, owner, pair).wait_recv()
        terms(owner, last=True)

    def halve(index):
        for j, copy in head_copies(index):
            copy.wait_recv()
            hpart[j - bits[index]] = hpart[j - bits[index]] + htook[j]
        if index + 1 < len(bits):
            for _, copy in head_copies(index + 1):
                copy.start()

    def out_copies(index):
        bit = bits[index]
        return [
            send(hout.at[j], hout.at[j + bit], o_send.at[j + bit], o_recv.at[j + bit], "head", flip(hme, bit))
            for j in range(0, n_head, 2 * bit)
        ]

    repeat(2, n - 1, collect)
    gathers[0].forward(pair, n - 1)
    for g in gathers[1:]:
        g.forward(me, 1)
    repeat(max(2, n - 1), n, collect)
    take_cross(z)
    attended()
    att_start()
    for g in gathers[1:]:
        repeat(2, n - 1, lambda s: g.forward(me, s))
    loads[7].wait()
    for b in range(qblk):
        prefill(b, 0)
        if b == 0:
            repeat(1, n - 1, att_forward)
            for g in gathers[1:]:
                g.forward(me, n - 1)
    att_forward(n - 1)
    project()
    for g in gathers[1:]:
        g.finish()
    append_all(me, qblk, owners_ref, kv, ak, av)
    for copy in slots:
        copy.start()
    rest = [(b, p) for p in range(1, kvh) for b in range(qblk)]
    halve(0)
    for b, p in rest[:1]:
        prefill(b, p)
    for index in range(1, len(bits)):
        halve(index)
    hout[0] = hpart[0].astype(bf16)
    for index in reversed(range(len(bits))):
        for copy in out_copies(index):
            copy.start()
        if index == len(bits) - 1:
            for b, p in rest[1:]:
                prefill(b, p)
        for copy in out_copies(index):
            copy.wait_recv()
    for j in range(n_head):
        chunk = hme
        for bit in bits:
            if j & bit:
                chunk = flip(chunk, bit)
        sample_ref[:, pl.ds(pl.multiple_of(chunk * columns, 128), columns)] = hout[j]

    for g in gathers:
        g.drain()

    def sent(d):
        cross_copy(d).wait_send()
        pl.when(d != z)(lambda: send(part.at[d, x], below.at[d], p_send.at[d], b_recv.at[d], "ctx", pair).wait_send())

    repeat(0, n, sent)
    for j in range(n):
        att_copy(j, me, pair).wait_send()
    for j in range(1, n):
        att_copy(n - 1 + j, line_at(j) + x, pair).wait_send()
    for index in range(len(bits)):
        for _, copy in head_copies(index):
            copy.wait_send()
        for copy in out_copies(index):
            copy.wait_send()
    for b in range(qblk):
        span_copy(b).wait()
    for copy in slots:
        copy.wait()


VM = pl.BlockSpec(memory_space=pltpu.VMEM)
SM = pl.BlockSpec(memory_space=pltpu.SMEM)
ANY = pl.BlockSpec(memory_space=pl.ANY)


def hand_over_kernel(*refs):
    count = len(refs) // 2
    for i in range(count):
        refs[count + i][...] = refs[i][...]


def hand_over(arrays):
    steps = 2
    specs = [pl.BlockSpec((a.shape[0] // steps, a.shape[1]), lambda i: (i, 0)) for a in arrays]
    return pl.pallas_call(
        hand_over_kernel,
        grid=(steps,),
        out_shape=tuple(jax.ShapeDtypeStruct(a.shape, a.dtype) for a in arrays),
        in_specs=specs,
        out_specs=tuple(specs),
        name="hand_over",
    )(*arrays)


def local(n_ctx, n_head, span_query, span_key, span_value, block_lists, owners, cache_key, cache_value, sample_query, sample_key, sample_value, out_weight):
    tokens = span_query.shape[0]
    kvh = span_key.shape[1] // HD
    group = span_query.shape[1] // HD // kvh
    qblk = tokens // BLOCK
    samples = sample_query.shape[0]
    per = kvh * group // n_ctx
    rows = per * samples
    resident = cache_key.shape[0]
    ksel = block_lists.shape[1]
    width = (ksel + 1) * BLOCK
    wide = kvh * HD
    columns = out_weight.shape[1] // n_head
    packet = rows + 8 * max(1, rows // 128)
    heads = 4
    n = n_ctx // 2
    slots = jax.ShapeDtypeStruct((MOST_BLOCKS * BLOCK, wide), bf16)
    dma = pltpu.SemaphoreType.DMA
    vm = pltpu.VMEM
    results = pl.pallas_call(
        functools.partial(layer_kernel, n_ctx, n_head, (samples, group, per, 512), (qblk, group, ksel, heads)),
        out_shape=(
            jax.ShapeDtypeStruct(span_query.shape, bf16),
            jax.ShapeDtypeStruct((samples, out_weight.shape[1]), bf16),
            slots,
            slots,
        ),
        in_specs=[SM, SM] + [ANY] * 11,
        out_specs=(ANY, VM, ANY, ANY),
        scratch_shapes=[
            vm(sample_query.shape, bf16),
            vm(span_key.shape, bf16),
            vm(span_value.shape, bf16),
            vm(sample_key.shape, bf16),
            vm(sample_value.shape, bf16),
            vm(cache_key.shape, bf16),
            vm(cache_value.shape, bf16),
            vm(span_query.shape, bf16),
            vm(out_weight.shape, bf16),
            [vm((n_ctx, 2, qblk, BLOCK, HD), bf16) for _ in range(kvh)],
            vm((2, rows, resident + tokens), f32),
            vm((group // heads, heads * BLOCK, width), f32),
            vm((width, 2 * HD), bf16),
            vm((width, HD), bf16),
            vm(span_query.shape, bf16),
            vm(slots.shape, bf16),
            vm(slots.shape, bf16),
            vm((n, 2, packet, HD), f32),
            vm((n, packet, HD), f32),
            vm((n, packet, HD), f32),
            vm((n, packet, HD), f32),
            vm((packet, HD), f32),
            vm((n_ctx, samples, per * HD), bf16),
            vm((n_head, samples, columns), f32),
            vm((n_head, samples, columns), f32),
            vm((n_head, samples, columns), bf16),
            dma((9 + 2 * kvh,)),
            dma((qblk + 2,)),
            [dma((3, n_ctx)) for _ in range(kvh)],
            [dma((n_ctx,)) for _ in range(kvh)],
            dma((n,)),
            dma((n,)),
            dma((n,)),
            dma((n,)),
            dma((n,)),
            dma((2 * n,)),
            dma((n_ctx,)),
            dma((n_head,)),
            dma((n_head,)),
            dma((n_head,)),
            dma((n_head,)),
        ],
        compiler_params=pltpu.CompilerParams(
            vmem_limit_bytes=60 << 20, collective_id=0, has_side_effects=True
        ),
        name="layer",
    )(
        block_lists.T,
        owners,
        sample_query,
        span_key,
        span_value,
        sample_key,
        sample_value,
        span_key.reshape(qblk, BLOCK, wide),
        span_value.reshape(qblk, BLOCK, wide),
        cache_key,
        cache_value,
        span_query,
        out_weight,
    )
    return hand_over(results)


def solution(mesh):
    c = P("ctx", "head")
    return jax.shard_map(
        functools.partial(local, mesh.shape["ctx"], mesh.shape["head"]),
        mesh=mesh,
        in_specs=(c, c, c, P(), P(), c, c, P(None, "head"), P(None, "head"), P(None, "head"), P("head", "ctx")),
        out_specs=(c, P(None, "ctx"), c, c),
        check_vma=False,
    )
```

```python
import functools

import jax
import jax.numpy as jnp
from jax import lax
from jax.experimental import pallas as pl
from jax.experimental.pallas import tpu as pltpu
from jax.sharding import PartitionSpec as P

HD = 128
BLOCK = 128
MOST_BLOCKS = 8
NEG = -1e30
SCALE = HD ** -0.5
EXP2_SCALE = SCALE * 1.4426950408889634
MESH = pl.DeviceIdType.MESH
bf16, f32 = jnp.bfloat16, jnp.float32


def dot_t(a, b):
    return lax.dot_general(a, b, (((1,), (1,)), ((), ())), preferred_element_type=f32)


def dot(a, b):
    return jnp.dot(a, b, preferred_element_type=f32)


def lane_fold(op, x):
    parts = [x[:, i * 128 : (i + 1) * 128] for i in range(x.shape[1] // 128)]
    while len(parts) > 1:
        parts = [op(*parts[i : i + 2]) if i + 1 < len(parts) else parts[i] for i in range(0, len(parts), 2)]
    return parts[0]


def column(ref, head, start, size):
    return ref[pl.ds(start, size), pl.ds(pl.multiple_of(head * HD, HD), HD)]


def flip(index, mask):
    return index + mask - 2 * mask * lax.rem(lax.div(index, mask), 2)


def pack_stats(m, l, rows):
    lane = lax.broadcasted_iota(jnp.int32, (rows, 128), 1)
    both = jnp.where(lane < 4, jnp.broadcast_to(m, (rows, 128)), jnp.broadcast_to(l, (rows, 128)))
    if rows < 128:
        both = jnp.concatenate([both] * (128 // rows), axis=0)
    slabs = [both[i * 128 : (i + 1) * 128].T[:8] for i in range(max(1, rows // 128))]
    return jnp.concatenate(slabs, axis=0)


def unpack_slab(slab):
    first = lax.broadcasted_iota(jnp.int32, (8, 128), 0) < 4
    swapped = pltpu.roll(slab, 4, 0)
    return jnp.where(first, slab, swapped), jnp.where(first, swapped, slab)


def spread(slab, rows):
    return jnp.concatenate([slab] * 16, axis=0).T[: min(rows, 128)]


def merge(rows, a, b, out):
    (a_ref, a_at), (b_ref, b_at), (out_ref, out_at) = a, b, out
    first = lax.broadcasted_iota(jnp.int32, (8, 128), 0) < 4
    for i in range(max(1, rows // 128)):
        stat = slice(rows + i * 8, rows + i * 8 + 8)
        part = slice(i * 128, min((i + 1) * 128, rows))
        ma, la = unpack_slab(a_ref[(*a_at, stat, slice(None))])
        mb, lb = unpack_slab(b_ref[(*b_at, stat, slice(None))])
        top = jnp.maximum(ma, mb)
        fa = jnp.exp2((ma - top) * EXP2_SCALE)
        fb = jnp.exp2((mb - top) * EXP2_SCALE)
        acc = spread(fa, rows) * a_ref[(*a_at, part, slice(None))] + spread(fb, rows) * b_ref[(*b_at, part, slice(None))]
        out_ref[(*out_at, part, slice(None))] = acc
        out_ref[(*out_at, stat, slice(None))] = jnp.where(first, top, fa * la + fb * lb)


def decode_scores(dims, tile, q_ref, ck_ref, sk_ref, s_ref):
    samples, group, per, chunk = dims
    head = lax.div(tile * per, group)
    q = jnp.concatenate([column(q_ref, tile * per + g, 0, samples) for g in range(per)], axis=0)
    resident = ck_ref.shape[0]
    high = None
    for c in range(resident // chunk):
        s = dot_t(q, column(ck_ref, head, c * chunk, chunk))
        s_ref[:, c * chunk : (c + 1) * chunk] = s
        top = lane_fold(jnp.maximum, s)
        high = top if high is None else jnp.maximum(high, top)
    s = dot_t(q, column(sk_ref, head, 0, sk_ref.shape[0]))
    s_ref[:, resident:] = s
    peaks = [jnp.max(high, axis=1, keepdims=True)]
    for b in range(sk_ref.shape[0] // BLOCK):
        peaks.append(jnp.max(s[:, b * BLOCK : (b + 1) * BLOCK], axis=1, keepdims=True))
    return peaks


def decode_values(dims, tile, peaks, cv_ref, sv_ref, s_ref):
    samples, group, per, chunk = dims
    rows = per * samples
    head = lax.div(tile * per, group)
    resident = cv_ref.shape[0]
    total, acc = None, jnp.zeros((rows, HD), f32)
    for c in range(resident // chunk):
        w = jnp.exp2((s_ref[:, c * chunk : (c + 1) * chunk] - peaks[0]) * EXP2_SCALE)
        some = lane_fold(jnp.add, w)
        total = some if total is None else total + some
        acc = acc + dot(w.astype(bf16), column(cv_ref, head, c * chunk, chunk))
    groups = [(peaks[0], jnp.sum(total, axis=1, keepdims=True), acc)]
    for b in range(sv_ref.shape[0] // BLOCK):
        at = resident + b * BLOCK
        w = jnp.exp2((s_ref[:, at : at + BLOCK] - peaks[b + 1]) * EXP2_SCALE)
        part = dot(w.astype(bf16), column(sv_ref, head, b * BLOCK, BLOCK))
        groups.append((peaks[b + 1], jnp.sum(w, axis=1, keepdims=True), part))
    top = functools.reduce(jnp.maximum, [g[0] for g in groups])
    factors = [jnp.exp2((g[0] - top) * EXP2_SCALE) for g in groups]
    total = sum(f * g[1] for f, g in zip(factors, groups))
    acc = sum(f * g[2] for f, g in zip(factors, groups))
    return top, total, acc


def prefill_unit(dims, own, b, k, lists_ref, q_ref, kv_ref, kc_ref, vc_ref, s_refs, out_ref):
    qblk, group, ksel, heads = dims
    rows, width = heads * BLOCK, (ksel + 1) * BLOCK
    row = lax.broadcasted_iota(jnp.int32, (BLOCK, BLOCK), 0)
    col = lax.broadcasted_iota(jnp.int32, (BLOCK, BLOCK), 1)
    one_hot = jnp.where(row == col, 1.0, 0.0).astype(bf16)
    late = jnp.where(row <= col, 0.0, NEG).astype(bf16)
    for i in range(ksel + 1):
        block = own if i == 0 else lists_ref[i - 1, own]
        holder, place = lax.div(block, qblk), lax.rem(block, qblk)
        here = slice(i * BLOCK, (i + 1) * BLOCK)
        kc_ref[here, :HD] = kv_ref[holder, 0, place]
        vc_ref[here, :] = kv_ref[holder, 1, place]
        if i == 0:
            kc_ref[here, HD:] = late
        else:
            kc_ref[here, HD:] = jnp.broadcast_to(jnp.where(block == own, NEG, 0.0), (BLOCK, BLOCK)).astype(bf16)
    tiles = group // heads
    cuts = [(0, 256), (256, 256), (512, width - 512)] if width > 512 else [(0, width)]
    peaks = []
    for t in range(tiles):
        q = jnp.concatenate([column(q_ref, k * group + t * heads + g, b * BLOCK, BLOCK) for g in range(heads)], axis=0)
        q = jnp.concatenate([q, jnp.concatenate([one_hot] * heads, axis=0)], axis=1)
        high = None
        for at, size in cuts:
            s = dot_t(q, kc_ref[at : at + size, :])
            s_refs[t, :, at : at + size] = s
            top = lane_fold(jnp.maximum, s)
            high = top if high is None else jnp.maximum(high, top)
        peaks.append(jnp.max(high, axis=1, keepdims=True))
    for t in range(tiles):
        total = None
        for at, size in cuts:
            w = jnp.exp2((s_refs[t, :, at : at + size] - peaks[t]) * EXP2_SCALE)
            s_refs[t, :, at : at + size] = w
            some = lane_fold(jnp.add, w)
            total = some if total is None else total + some
        inverse = 1.0 / jnp.sum(total, axis=1, keepdims=True)
        probs = (s_refs[t, :, :] * inverse).astype(bf16)
        out = dot(probs, vc_ref[...]).astype(bf16)
        for g in range(heads):
            at = (k * group + t * heads + g) * HD
            out_ref[b * BLOCK : (b + 1) * BLOCK, at : at + HD] = out[g * BLOCK : (g + 1) * BLOCK]


def append_all(position, qblk, owners_ref, kv_refs, ak_ref, av_ref):
    blocks = owners_ref.shape[0]

    def count(b, carry):
        rank, picked = carry
        mine = owners_ref[b] == position
        picked = tuple(jnp.where(mine & (rank == slot), b, p) for slot, p in enumerate(picked))
        return rank + mine.astype(jnp.int32), picked

    rank, picked = lax.fori_loop(
        0, blocks, count, (jnp.int32(0), tuple(jnp.int32(0) for _ in range(MOST_BLOCKS)))
    )
    for slot in range(MOST_BLOCKS):
        live = jnp.broadcast_to(rank, (BLOCK, HD)) > slot
        holder, place = lax.div(picked[slot], qblk), lax.rem(picked[slot], qblk)
        for k, kv_ref in enumerate(kv_refs):
            for kind, dst in enumerate((ak_ref, av_ref)):
                x = kv_ref[holder, kind, place].astype(f32)
                dst[slot * BLOCK : (slot + 1) * BLOCK, k * HD : (k + 1) * HD] = jnp.where(live, x, 0.0).astype(bf16)


def repeat(low, high, body):
    if high - low <= 4:
        for i in range(low, high):
            body(i)
    else:

        def step(i, carry):
            body(i)
            return carry

        lax.fori_loop(low, high, step, 0)


def layer_kernel(n_ctx, n_head, dims, pre_dims, *refs):
    (lists_ref, owners_ref, q_hbm, sk_hbm, sv_hbm, ok_hbm, ov_hbm, span_k, span_v, ck_hbm, cv_hbm, sq_hbm, w_hbm) = refs[:13]
    (span_hbm, sample_ref, ak_hbm, av_hbm) = refs[13:17]
    (q_ref, sk_ref, sv_ref, ok_ref, ov_ref, ck, cv, sq, w, kv, s_ref, pre_s, kc, vc, out_v, ak, av) = refs[17:34]
    (part, below, above, cross, fresh, att, hpart, htook, hout) = refs[34:43]
    (in_sem, out_sem, g_send, g_recv, p_send, b_recv, a_recv, c_send, c_recv, t_send, t_recv, h_send, h_recv, o_send, o_recv) = refs[43:]
    samples, group, per, _ = dims
    qblk, _, ksel, _ = pre_dims
    rows = per * samples
    kvh = len(kv)
    me = lax.axis_index("ctx")
    hme = lax.axis_index("head")
    n = n_ctx // 2
    z, x = lax.div(me, 2), lax.rem(me, 2)
    pair = z * 2 + 1 - x
    bits = [1 << i for i in range(n_head.bit_length() - 1)]

    def local(index, src, dst):
        return pltpu.make_async_copy(src, dst, in_sem.at[index])

    loads = [
        local(i, a, b)
        for i, (a, b) in enumerate(
            (
                (q_hbm, q_ref),
                (ck_hbm, ck),
                (cv_hbm, cv),
                (sk_hbm, sk_ref),
                (sv_hbm, sv_ref),
                (ok_hbm, ok_ref),
                (ov_hbm, ov_ref),
                (sq_hbm, sq),
                (w_hbm, w),
            )
        )
    ]
    mine = [
        local(9 + p * 2 + kind, src.at[:, :, pl.ds(p * HD, HD)], kv[p].at[me, kind])
        for p in range(kvh)
        for kind, src in enumerate((span_k, span_v))
    ]
    for copy in mine + loads[:7]:
        copy.start()

    barrier = pltpu.get_barrier_semaphore()
    for j in range(1, n):
        pl.semaphore_signal(barrier, inc=1, device_id={"ctx": lax.rem(z + j, n) * 2 + x}, device_id_type=MESH)
    pl.semaphore_signal(barrier, inc=1, device_id={"ctx": pair}, device_id_type=MESH)
    for bit in bits:
        pl.semaphore_signal(barrier, inc=1, device_id={"head": flip(hme, bit)}, device_id_type=MESH)
    pl.semaphore_wait(barrier, n + len(bits))
    for copy in mine:
        copy.wait()

    def send(src, dst, ssem, rsem, axis, to):
        return pltpu.make_async_remote_copy(
            src_ref=src, dst_ref=dst, send_sem=ssem, recv_sem=rsem, device_id={axis: to}, device_id_type=MESH
        )

    class Line:
        def __init__(self, buf, ssem, rsem, pair_first):
            self.buf, self.ssem, self.rsem, self.pair_first = buf, ssem, rsem, pair_first

        def copy(self, owner, way, to):
            view = self.buf.at[owner]
            return send(view, view, self.ssem.at[way, owner], self.rsem.at[owner], "ctx", to)

        def landed(self, owner):
            self.copy(owner, 0, pair).wait_recv()

        def up(self, owner, act):
            pl.when(z + 1 < n)(lambda: act(self.copy(owner, 1, me + 2)))

        def down(self, owner, act):
            pl.when(z > 0)(lambda: act(self.copy(owner, 2, me - 2)))

        def own(self, act):
            act(self.copy(me, 0, pair))
            self.up(me, act)
            self.down(me, act)

        def paired(self, act):
            if self.pair_first:
                self.up(pair, act)
                self.down(pair, act)

        def hops(self, base, s, act):
            def from_below():
                if not self.pair_first:
                    act(self.copy(base - 2 * s, 0, pair))
                self.up(base - 2 * s, act)

            def from_above():
                if not self.pair_first:
                    act(self.copy(base + 2 * s, 0, pair))
                self.down(base + 2 * s, act)

            pl.when(z - s >= 0)(from_below)
            pl.when(z + s < n)(from_above)

        def start(self):
            self.own(lambda c: c.start())

        def forward_pair(self):
            self.landed(pair)
            self.paired(lambda c: c.start())

        def forward(self, base, s):
            pl.when(z - s >= 0)(lambda: self.landed(base - 2 * s))
            pl.when(z + s < n)(lambda: self.landed(base + 2 * s))
            self.hops(base, s, lambda c: c.start())

        def finish(self):
            repeat(0, n, lambda j: self.landed(j * 2 + 1 - x))

        def drain(self):
            def done(c):
                c.wait_send()

            self.own(done)
            self.paired(done)
            for base in (me, pair) if self.pair_first else (me,):
                repeat(1, n, lambda s: self.hops(base, s, done))

    gathers = [Line(kv[p], g_send[p], g_recv[p], p == 0) for p in range(kvh)]
    gathers[0].start()

    for i in (0, 5, 6):
        loads[i].wait()
    key_head = lax.div(me * per, group)
    own_key = column(ok_ref, key_head, 0, samples).astype(f32)
    own = [
        jnp.sum(column(q_ref, me * per + g, 0, samples).astype(f32) * own_key, axis=1, keepdims=True)
        for g in range(per)
    ]
    fresh[:rows, :] = jnp.concatenate([column(ov_ref, key_head, 0, samples).astype(f32)] * per, axis=0)
    fresh[rows:, :] = pack_stats(jnp.concatenate(own, axis=0), jnp.ones((rows, 1), f32), rows)
    for i in (1, 2, 3, 4):
        loads[i].wait()
    loads[7].start()
    loads[8].start()

    def cross_copy(d):
        return send(part.at[d, 1 - x], cross.at[d], c_send.at[d], c_recv.at[d], "ctx", pair)

    def up_copy(d):
        return send(part.at[d, x], below.at[d], p_send.at[d], b_recv.at[d], "ctx", me + 2)

    def down_copy(d):
        return send(part.at[d, x], above.at[d], p_send.at[d], a_recv.at[d], "ctx", me - 2)

    way = 2 * lax.div(z, n // 2) - 1

    def unit_at(i):
        return lax.rem(z + way * (1 + i) + 2 * n, n)

    def take_cross(d):
        cross_copy(d).wait_recv()
        merge(rows, (part, (d, x)), (cross, (d,)), (part, (d, x)))

    def collect(r):
        def from_below():
            d = n - 1 - r + z
            send(part.at[d, x], below.at[d], p_send.at[d], b_recv.at[d], "ctx", pair).wait_recv()
            merge(rows, (part, (d, x)), (below, (d,)), (part, (d, x)))
            pl.when(d > z)(lambda: up_copy(d).start())

        def from_above():
            d = r - (n - 1) + z
            send(part.at[d, x], above.at[d], p_send.at[d], a_recv.at[d], "ctx", pair).wait_recv()
            merge(rows, (part, (d, x)), (above, (d,)), (part, (d, x)))
            pl.when(d < z)(lambda: down_copy(d).start())

        pl.when((z > 0) & (r >= z))(from_below)
        pl.when((z < n - 1) & (r + z >= n - 1))(from_above)

    def decode_step(i, carry):
        d = unit_at(i)
        peaks = [decode_scores(dims, d * 2 + t, q_ref, ck, sk_ref, s_ref.at[t]) for t in range(2)]
        for t in range(2):
            m, l, acc = decode_values(dims, d * 2 + t, peaks[t], cv, sv_ref, s_ref.at[t])
            part[d, t, :rows, :] = acc
            part[d, t, rows:, :] = pack_stats(m, l, rows)
        cross_copy(d).start()

        @pl.when(i >= 1)
        def _():
            before = unit_at(i - 1)
            take_cross(before)
            pl.when(z == 0)(lambda: up_copy(before).start())
            pl.when(z == n - 1)(lambda: down_copy(before).start())

        @pl.when(i == 0)
        def _():
            gathers[0].forward_pair()

        @pl.when((i >= 1) & (i < n - 1))
        def _():
            gathers[0].forward(pair, i)

        @pl.when(i < n - 1)
        def _():
            gathers[0].forward(me, i + 1)

        @pl.when(i == n - 2)
        def _():
            collect(1)

        @pl.when(i == 1)
        def _():
            for g in gathers[1:]:
                g.start()

        return carry

    lax.fori_loop(0, n, decode_step, 0)

    def prefill(b, p):
        prefill_unit(pre_dims, me * qblk + b, b, p, lists_ref, sq, kv[p], kc, vc, pre_s, out_v)
        if p == kvh - 1:
            span_copy(b).start()

    def span_copy(b):
        where = pl.ds(b * BLOCK, BLOCK)
        return pltpu.make_async_copy(out_v.at[where], span_hbm.at[where], out_sem.at[b])

    slots = [
        pltpu.make_async_copy(ak, ak_hbm, out_sem.at[qblk]),
        pltpu.make_async_copy(av, av_hbm, out_sem.at[qblk + 1]),
    ]

    def attended():
        merge(rows, (part, (z, x)), (fresh, ()), (fresh, ()))
        for i in range(max(1, rows // 128)):
            size = min(rows, 128)
            _, l = unpack_slab(fresh[rows + i * 8 : rows + i * 8 + 8, :])
            done = (fresh[i * 128 : i * 128 + size, :] * spread(1.0 / l, rows)).astype(bf16)
            for g in range(size // samples):
                head = i * (128 // samples) + g
                att[me, :, head * HD : (head + 1) * HD] = done[g * samples : (g + 1) * samples]

    columns = w.shape[1] // n_head
    depth = per * HD

    def att_copy(index, owner, to):
        view = att.at[owner]
        return send(view, view, t_send.at[index], t_recv.at[owner], "ctx", to)

    def line_at(j):
        return lax.rem(z - j + n, n) * 2

    def att_start():
        att_copy(0, me, pair).start()
        for j in range(1, n):
            att_copy(j, me, lax.rem(z + j, n) * 2 + x).start()

    def head_copies(index):
        bit = bits[index]
        return [
            (j, send(hpart.at[j], htook.at[j], h_send.at[j], h_recv.at[j], "head", flip(hme, bit)))
            for j in range(bit, n_head, 2 * bit)
        ]

    def terms(owner, first=False, last=False):
        order = sorted(range(n_head), key=lambda j: [1 - (j & bit) // bit for bit in bits])
        starts = dict(head_copies(0)) if last else {}
        for j in order:
            chunk = hme
            for bit in bits:
                if j & bit:
                    chunk = flip(chunk, bit)
            where = pl.ds(pl.multiple_of(chunk * columns, 128), columns)
            x = dot(att[owner], w[pl.ds(pl.multiple_of(owner * depth, 128), depth), where])
            hpart[j] = x if first else hpart[j] + x
            if j in starts:
                starts[j].start()

    def att_forward(j):
        owner = line_at(j) + x
        att_copy(0, owner, pair).wait_recv()
        att_copy(n - 1 + j, owner, pair).start()

    def project():
        loads[8].wait()
        terms(me, first=True)

        def straight(j):
            terms(line_at(j) + x)

        def paired(j):
            owner = line_at(j) + 1 - x
            att_copy(0, owner, pair).wait_recv()
            terms(owner)

        repeat(1, n, straight)
        repeat(0, n - 1, paired)
        owner = line_at(n - 1) + 1 - x
        att_copy(0, owner, pair).wait_recv()
        terms(owner, last=True)

    def halve(index):
        for j, copy in head_copies(index):
            copy.wait_recv()
            hpart[j - bits[index]] = hpart[j - bits[index]] + htook[j]
        if index + 1 < len(bits):
            for _, copy in head_copies(index + 1):
                copy.start()

    def out_copies(index):
        bit = bits[index]
        return [
            send(hout.at[j], hout.at[j + bit], o_send.at[j + bit], o_recv.at[j + bit], "head", flip(hme, bit))
            for j in range(0, n_head, 2 * bit)
        ]

    repeat(2, n - 1, collect)
    gathers[0].forward(pair, n - 1)
    for g in gathers[1:]:
        g.forward(me, 1)
    repeat(max(2, n - 1), n, collect)
    take_cross(z)
    attended()
    att_start()
    for g in gathers[1:]:
        repeat(2, n - 1, lambda s: g.forward(me, s))
    loads[7].wait()
    for b in range(qblk):
        prefill(b, 0)
        if b == 0:
            repeat(1, n - 1, att_forward)
            att_forward(n - 1)
            for g in gathers[1:]:
                g.forward(me, n - 1)
            project()
    halve(0)
    for g in gathers[1:]:
        g.finish()
    append_all(me, qblk, owners_ref, kv, ak, av)
    for copy in slots:
        copy.start()
    rest = [(b, p) for p in range(1, kvh) for b in range(qblk)]
    for b, p in rest[:1]:
        prefill(b, p)
    for index in range(1, len(bits)):
        halve(index)
    hout[0] = hpart[0].astype(bf16)
    for index in reversed(range(len(bits))):
        for copy in out_copies(index):
            copy.start()
        if index == len(bits) - 1:
            for b, p in rest[1:]:
                prefill(b, p)
        for copy in out_copies(index):
            copy.wait_recv()
    for j in range(n_head):
        chunk = hme
        for bit in bits:
            if j & bit:
                chunk = flip(chunk, bit)
        sample_ref[:, pl.ds(pl.multiple_of(chunk * columns, 128), columns)] = hout[j]

    for g in gathers:
        g.drain()

    def sent(d):
        cross_copy(d).wait_send()
        pl.when(d != z)(lambda: send(part.at[d, x], below.at[d], p_send.at[d], b_recv.at[d], "ctx", pair).wait_send())

    repeat(0, n, sent)
    for j in range(n):
        att_copy(j, me, pair).wait_send()
    for j in range(1, n):
        att_copy(n - 1 + j, line_at(j) + x, pair).wait_send()
    for index in range(len(bits)):
        for _, copy in head_copies(index):
            copy.wait_send()
        for copy in out_copies(index):
            copy.wait_send()
    for b in range(qblk):
        span_copy(b).wait()
    for copy in slots:
        copy.wait()


VM = pl.BlockSpec(memory_space=pltpu.VMEM)
SM = pl.BlockSpec(memory_space=pltpu.SMEM)
ANY = pl.BlockSpec(memory_space=pl.ANY)


def hand_over_kernel(*refs):
    count = len(refs) // 2
    for i in range(count):
        refs[count + i][...] = refs[i][...]


def hand_over(arrays):
    steps = 2
    specs = [pl.BlockSpec((a.shape[0] // steps, a.shape[1]), lambda i: (i, 0)) for a in arrays]
    return pl.pallas_call(
        hand_over_kernel,
        grid=(steps,),
        out_shape=tuple(jax.ShapeDtypeStruct(a.shape, a.dtype) for a in arrays),
        in_specs=specs,
        out_specs=tuple(specs),
        name="hand_over",
    )(*arrays)


def local(n_ctx, n_head, span_query, span_key, span_value, block_lists, owners, cache_key, cache_value, sample_query, sample_key, sample_value, out_weight):
    tokens = span_query.shape[0]
    kvh = span_key.shape[1] // HD
    group = span_query.shape[1] // HD // kvh
    qblk = tokens // BLOCK
    samples = sample_query.shape[0]
    per = kvh * group // n_ctx
    rows = per * samples
    resident = cache_key.shape[0]
    ksel = block_lists.shape[1]
    width = (ksel + 1) * BLOCK
    wide = kvh * HD
    columns = out_weight.shape[1] // n_head
    packet = rows + 8 * max(1, rows // 128)
    heads = 4
    n = n_ctx // 2
    slots = jax.ShapeDtypeStruct((MOST_BLOCKS * BLOCK, wide), bf16)
    dma = pltpu.SemaphoreType.DMA
    vm = pltpu.VMEM
    results = pl.pallas_call(
        functools.partial(layer_kernel, n_ctx, n_head, (samples, group, per, 512), (qblk, group, ksel, heads)),
        out_shape=(
            jax.ShapeDtypeStruct(span_query.shape, bf16),
            jax.ShapeDtypeStruct((samples, out_weight.shape[1]), bf16),
            slots,
            slots,
        ),
        in_specs=[SM, SM] + [ANY] * 11,
        out_specs=(ANY, VM, ANY, ANY),
        scratch_shapes=[
            vm(sample_query.shape, bf16),
            vm(span_key.shape, bf16),
            vm(span_value.shape, bf16),
            vm(sample_key.shape, bf16),
            vm(sample_value.shape, bf16),
            vm(cache_key.shape, bf16),
            vm(cache_value.shape, bf16),
            vm(span_query.shape, bf16),
            vm(out_weight.shape, bf16),
            [vm((n_ctx, 2, qblk, BLOCK, HD), bf16) for _ in range(kvh)],
            vm((2, rows, resident + tokens), f32),
            vm((group // heads, heads * BLOCK, width), f32),
            vm((width, 2 * HD), bf16),
            vm((width, HD), bf16),
            vm(span_query.shape, bf16),
            vm(slots.shape, bf16),
            vm(slots.shape, bf16),
            vm((n, 2, packet, HD), f32),
            vm((n, packet, HD), f32),
            vm((n, packet, HD), f32),
            vm((n, packet, HD), f32),
            vm((packet, HD), f32),
            vm((n_ctx, samples, per * HD), bf16),
            vm((n_head, samples, columns), f32),
            vm((n_head, samples, columns), f32),
            vm((n_head, samples, columns), bf16),
            dma((9 + 2 * kvh,)),
            dma((qblk + 2,)),
            [dma((3, n_ctx)) for _ in range(kvh)],
            [dma((n_ctx,)) for _ in range(kvh)],
            dma((n,)),
            dma((n,)),
            dma((n,)),
            dma((n,)),
            dma((n,)),
            dma((2 * n,)),
            dma((n_ctx,)),
            dma((n_head,)),
            dma((n_head,)),
            dma((n_head,)),
            dma((n_head,)),
        ],
        compiler_params=pltpu.CompilerParams(
            vmem_limit_bytes=60 << 20, collective_id=0, has_side_effects=True
        ),
        name="layer",
    )(
        block_lists.T,
        owners,
        sample_query,
        span_key,
        span_value,
        sample_key,
        sample_value,
        span_key.reshape(qblk, BLOCK, wide),
        span_value.reshape(qblk, BLOCK, wide),
        cache_key,
        cache_value,
        span_query,
        out_weight,
    )
    return hand_over(results)


def solution(mesh):
    c = P("ctx", "head")
    return jax.shard_map(
        functools.partial(local, mesh.shape["ctx"], mesh.shape["head"]),
        mesh=mesh,
        in_specs=(c, c, c, P(), P(), c, c, P(None, "head"), P(None, "head"), P(None, "head"), P("head", "ctx")),
        out_specs=(c, P(None, "ctx"), c, c),
        check_vma=False,
    )
```

```python
import functools

import jax
import jax.numpy as jnp
from jax import lax
from jax.experimental import pallas as pl
from jax.experimental.pallas import tpu as pltpu
from jax.sharding import PartitionSpec as P

HD = 128
BLOCK = 128
MOST_BLOCKS = 8
NEG = -1e30
SCALE = HD ** -0.5
EXP2_SCALE = SCALE * 1.4426950408889634
MESH = pl.DeviceIdType.MESH
bf16, f32 = jnp.bfloat16, jnp.float32


def dot_t(a, b):
    return lax.dot_general(a, b, (((1,), (1,)), ((), ())), preferred_element_type=f32)


def dot(a, b):
    return jnp.dot(a, b, preferred_element_type=f32)


def lane_fold(op, x):
    parts = [x[:, i * 128 : (i + 1) * 128] for i in range(x.shape[1] // 128)]
    while len(parts) > 1:
        parts = [op(*parts[i : i + 2]) if i + 1 < len(parts) else parts[i] for i in range(0, len(parts), 2)]
    return parts[0]


def column(ref, head, start, size):
    return ref[pl.ds(start, size), pl.ds(pl.multiple_of(head * HD, HD), HD)]


def flip(index, mask):
    return index + mask - 2 * mask * lax.rem(lax.div(index, mask), 2)


def pack_stats(m, l, rows):
    lane = lax.broadcasted_iota(jnp.int32, (rows, 128), 1)
    both = jnp.where(lane < 4, jnp.broadcast_to(m, (rows, 128)), jnp.broadcast_to(l, (rows, 128)))
    if rows < 128:
        both = jnp.concatenate([both] * (128 // rows), axis=0)
    slabs = [both[i * 128 : (i + 1) * 128].T[:8] for i in range(max(1, rows // 128))]
    return jnp.concatenate(slabs, axis=0)


def unpack_slab(slab):
    first = lax.broadcasted_iota(jnp.int32, (8, 128), 0) < 4
    swapped = pltpu.roll(slab, 4, 0)
    return jnp.where(first, slab, swapped), jnp.where(first, swapped, slab)


def spread(slab, rows):
    return jnp.concatenate([slab] * 16, axis=0).T[: min(rows, 128)]


def merge(rows, a, b, out):
    (a_ref, a_at), (b_ref, b_at), (out_ref, out_at) = a, b, out
    first = lax.broadcasted_iota(jnp.int32, (8, 128), 0) < 4
    for i in range(max(1, rows // 128)):
        stat = slice(rows + i * 8, rows + i * 8 + 8)
        part = slice(i * 128, min((i + 1) * 128, rows))
        ma, la = unpack_slab(a_ref[(*a_at, stat, slice(None))])
        mb, lb = unpack_slab(b_ref[(*b_at, stat, slice(None))])
        top = jnp.maximum(ma, mb)
        fa = jnp.exp2((ma - top) * EXP2_SCALE)
        fb = jnp.exp2((mb - top) * EXP2_SCALE)
        acc = spread(fa, rows) * a_ref[(*a_at, part, slice(None))] + spread(fb, rows) * b_ref[(*b_at, part, slice(None))]
        out_ref[(*out_at, part, slice(None))] = acc
        out_ref[(*out_at, stat, slice(None))] = jnp.where(first, top, fa * la + fb * lb)


def decode_scores(dims, tile, q_ref, ck_ref, sk_ref, s_ref):
    samples, group, per, chunk = dims
    head = lax.div(tile * per, group)
    q = jnp.concatenate([column(q_ref, tile * per + g, 0, samples) for g in range(per)], axis=0)
    resident = ck_ref.shape[0]
    high = None
    for c in range(resident // chunk):
        s = dot_t(q, column(ck_ref, head, c * chunk, chunk))
        s_ref[:, c * chunk : (c + 1) * chunk] = s
        top = lane_fold(jnp.maximum, s)
        high = top if high is None else jnp.maximum(high, top)
    s = dot_t(q, column(sk_ref, head, 0, sk_ref.shape[0]))
    s_ref[:, resident:] = s
    peaks = [jnp.max(high, axis=1, keepdims=True)]
    for b in range(sk_ref.shape[0] // BLOCK):
        peaks.append(jnp.max(s[:, b * BLOCK : (b + 1) * BLOCK], axis=1, keepdims=True))
    return peaks


def decode_values(dims, tile, peaks, cv_ref, sv_ref, s_ref):
    samples, group, per, chunk = dims
    rows = per * samples
    head = lax.div(tile * per, group)
    resident = cv_ref.shape[0]
    total, acc = None, jnp.zeros((rows, HD), f32)
    for c in range(resident // chunk):
        w = jnp.exp2((s_ref[:, c * chunk : (c + 1) * chunk] - peaks[0]) * EXP2_SCALE)
        some = lane_fold(jnp.add, w)
        total = some if total is None else total + some
        acc = acc + dot(w.astype(bf16), column(cv_ref, head, c * chunk, chunk))
    groups = [(peaks[0], jnp.sum(total, axis=1, keepdims=True), acc)]
    for b in range(sv_ref.shape[0] // BLOCK):
        at = resident + b * BLOCK
        w = jnp.exp2((s_ref[:, at : at + BLOCK] - peaks[b + 1]) * EXP2_SCALE)
        part = dot(w.astype(bf16), column(sv_ref, head, b * BLOCK, BLOCK))
        groups.append((peaks[b + 1], jnp.sum(w, axis=1, keepdims=True), part))
    top = functools.reduce(jnp.maximum, [g[0] for g in groups])
    factors = [jnp.exp2((g[0] - top) * EXP2_SCALE) for g in groups]
    total = sum(f * g[1] for f, g in zip(factors, groups))
    acc = sum(f * g[2] for f, g in zip(factors, groups))
    return top, total, acc


def prefill_unit(dims, own, b, k, lists_ref, q_ref, kv_ref, kc_ref, vc_ref, s_refs, out_ref):
    qblk, group, ksel, heads = dims
    rows, width = heads * BLOCK, (ksel + 1) * BLOCK
    row = lax.broadcasted_iota(jnp.int32, (BLOCK, BLOCK), 0)
    col = lax.broadcasted_iota(jnp.int32, (BLOCK, BLOCK), 1)
    one_hot = jnp.where(row == col, 1.0, 0.0).astype(bf16)
    late = jnp.where(row <= col, 0.0, NEG).astype(bf16)
    for i in range(ksel + 1):
        block = own if i == 0 else lists_ref[i - 1, own]
        holder, place = lax.div(block, qblk), lax.rem(block, qblk)
        here = slice(i * BLOCK, (i + 1) * BLOCK)
        kc_ref[here, :HD] = kv_ref[holder, 0, place]
        vc_ref[here, :] = kv_ref[holder, 1, place]
        if i == 0:
            kc_ref[here, HD:] = late
        else:
            kc_ref[here, HD:] = jnp.broadcast_to(jnp.where(block == own, NEG, 0.0), (BLOCK, BLOCK)).astype(bf16)
    tiles = group // heads
    cuts = [(0, 256), (256, 256), (512, width - 512)] if width > 512 else [(0, width)]
    peaks = []
    for t in range(tiles):
        q = jnp.concatenate([column(q_ref, k * group + t * heads + g, b * BLOCK, BLOCK) for g in range(heads)], axis=0)
        q = jnp.concatenate([q, jnp.concatenate([one_hot] * heads, axis=0)], axis=1)
        high = None
        for at, size in cuts:
            s = dot_t(q, kc_ref[at : at + size, :])
            s_refs[t, :, at : at + size] = s
            top = lane_fold(jnp.maximum, s)
            high = top if high is None else jnp.maximum(high, top)
        peaks.append(jnp.max(high, axis=1, keepdims=True))
    for t in range(tiles):
        total = None
        for at, size in cuts:
            w = jnp.exp2((s_refs[t, :, at : at + size] - peaks[t]) * EXP2_SCALE)
            s_refs[t, :, at : at + size] = w
            some = lane_fold(jnp.add, w)
            total = some if total is None else total + some
        inverse = 1.0 / jnp.sum(total, axis=1, keepdims=True)
        probs = (s_refs[t, :, :] * inverse).astype(bf16)
        out = dot(probs, vc_ref[...]).astype(bf16)
        for g in range(heads):
            at = (k * group + t * heads + g) * HD
            out_ref[b * BLOCK : (b + 1) * BLOCK, at : at + HD] = out[g * BLOCK : (g + 1) * BLOCK]


def append_all(position, qblk, owners_ref, kv_refs, ak_ref, av_ref):
    blocks = owners_ref.shape[0]

    def count(b, carry):
        rank, picked = carry
        mine = owners_ref[b] == position
        picked = tuple(jnp.where(mine & (rank == slot), b, p) for slot, p in enumerate(picked))
        return rank + mine.astype(jnp.int32), picked

    rank, picked = lax.fori_loop(
        0, blocks, count, (jnp.int32(0), tuple(jnp.int32(0) for _ in range(MOST_BLOCKS)))
    )
    for slot in range(MOST_BLOCKS):
        live = jnp.broadcast_to(rank, (BLOCK, HD)) > slot
        holder, place = lax.div(picked[slot], qblk), lax.rem(picked[slot], qblk)
        for k, kv_ref in enumerate(kv_refs):
            for kind, dst in enumerate((ak_ref, av_ref)):
                x = kv_ref[holder, kind, place].astype(f32)
                dst[slot * BLOCK : (slot + 1) * BLOCK, k * HD : (k + 1) * HD] = jnp.where(live, x, 0.0).astype(bf16)


def repeat(low, high, body):
    if high - low <= 4:
        for i in range(low, high):
            body(i)
    else:

        def step(i, carry):
            body(i)
            return carry

        lax.fori_loop(low, high, step, 0)


def layer_kernel(n_ctx, n_head, dims, pre_dims, *refs):
    (lists_ref, owners_ref, q_hbm, sk_hbm, sv_hbm, ok_hbm, ov_hbm, span_k, span_v, ck_hbm, cv_hbm, sq_hbm, w_hbm) = refs[:13]
    (span_hbm, sample_ref, ak_hbm, av_hbm) = refs[13:17]
    (q_ref, sk_ref, sv_ref, ok_ref, ov_ref, ck, cv, sq, w, kv, s_ref, pre_s, kc, vc, out_v, ak, av) = refs[17:34]
    (part, below, above, cross, fresh, att, hpart, htook, hout) = refs[34:43]
    (in_sem, out_sem, g_send, g_recv, p_send, b_recv, a_recv, c_send, c_recv, t_send, t_recv, h_send, h_recv, o_send, o_recv) = refs[43:]
    samples, group, per, _ = dims
    qblk, _, ksel, _ = pre_dims
    rows = per * samples
    kvh = len(kv)
    me = lax.axis_index("ctx")
    hme = lax.axis_index("head")
    n = n_ctx // 2
    z, x = lax.div(me, 2), lax.rem(me, 2)
    pair = z * 2 + 1 - x
    bits = [1 << i for i in range(n_head.bit_length() - 1)]

    def local(index, src, dst):
        return pltpu.make_async_copy(src, dst, in_sem.at[index])

    loads = [
        local(i, a, b)
        for i, (a, b) in enumerate(
            (
                (q_hbm, q_ref),
                (ck_hbm, ck),
                (cv_hbm, cv),
                (sk_hbm, sk_ref),
                (sv_hbm, sv_ref),
                (ok_hbm, ok_ref),
                (ov_hbm, ov_ref),
                (sq_hbm, sq),
                (w_hbm, w),
            )
        )
    ]
    mine = [
        local(9 + p * 2 + kind, src.at[:, :, pl.ds(p * HD, HD)], kv[p].at[me, kind])
        for p in range(kvh)
        for kind, src in enumerate((span_k, span_v))
    ]
    for copy in mine + loads[:7]:
        copy.start()

    barrier = pltpu.get_barrier_semaphore()
    for j in range(1, n):
        pl.semaphore_signal(barrier, inc=1, device_id={"ctx": lax.rem(z + j, n) * 2 + x}, device_id_type=MESH)
    pl.semaphore_signal(barrier, inc=1, device_id={"ctx": pair}, device_id_type=MESH)
    for bit in bits:
        pl.semaphore_signal(barrier, inc=1, device_id={"head": flip(hme, bit)}, device_id_type=MESH)
    pl.semaphore_wait(barrier, n + len(bits))
    for copy in mine:
        copy.wait()

    def send(src, dst, ssem, rsem, axis, to):
        return pltpu.make_async_remote_copy(
            src_ref=src, dst_ref=dst, send_sem=ssem, recv_sem=rsem, device_id={axis: to}, device_id_type=MESH
        )

    class Line:
        def __init__(self, buf, ssem, rsem, pair_first):
            self.buf, self.ssem, self.rsem, self.pair_first = buf, ssem, rsem, pair_first

        def copy(self, owner, way, to):
            view = self.buf.at[owner]
            return send(view, view, self.ssem.at[way, owner], self.rsem.at[owner], "ctx", to)

        def landed(self, owner):
            self.copy(owner, 0, pair).wait_recv()

        def up(self, owner, act):
            pl.when(z + 1 < n)(lambda: act(self.copy(owner, 1, me + 2)))

        def down(self, owner, act):
            pl.when(z > 0)(lambda: act(self.copy(owner, 2, me - 2)))

        def own(self, act):
            act(self.copy(me, 0, pair))
            self.up(me, act)
            self.down(me, act)

        def paired(self, act):
            if self.pair_first:
                self.up(pair, act)
                self.down(pair, act)

        def hops(self, base, s, act):
            def from_below():
                if not self.pair_first:
                    act(self.copy(base - 2 * s, 0, pair))
                self.up(base - 2 * s, act)

            def from_above():
                if not self.pair_first:
                    act(self.copy(base + 2 * s, 0, pair))
                self.down(base + 2 * s, act)

            pl.when(z - s >= 0)(from_below)
            pl.when(z + s < n)(from_above)

        def start(self):
            self.own(lambda c: c.start())

        def forward_pair(self):
            self.landed(pair)
            self.paired(lambda c: c.start())

        def forward(self, base, s):
            pl.when(z - s >= 0)(lambda: self.landed(base - 2 * s))
            pl.when(z + s < n)(lambda: self.landed(base + 2 * s))
            self.hops(base, s, lambda c: c.start())

        def finish(self):
            repeat(0, n, lambda j: self.landed(j * 2 + 1 - x))

        def drain(self):
            def done(c):
                c.wait_send()

            self.own(done)
            self.paired(done)
            for base in (me, pair) if self.pair_first else (me,):
                repeat(1, n, lambda s: self.hops(base, s, done))

    gathers = [Line(kv[p], g_send[p], g_recv[p], p == 0) for p in range(kvh)]
    gathers[0].start()

    for i in (0, 5, 6):
        loads[i].wait()
    key_head = lax.div(me * per, group)
    own_key = column(ok_ref, key_head, 0, samples).astype(f32)
    own = [
        jnp.sum(column(q_ref, me * per + g, 0, samples).astype(f32) * own_key, axis=1, keepdims=True)
        for g in range(per)
    ]
    fresh[:rows, :] = jnp.concatenate([column(ov_ref, key_head, 0, samples).astype(f32)] * per, axis=0)
    fresh[rows:, :] = pack_stats(jnp.concatenate(own, axis=0), jnp.ones((rows, 1), f32), rows)
    for i in (1, 2, 3, 4):
        loads[i].wait()
    loads[7].start()
    loads[8].start()

    def cross_copy(d):
        return send(part.at[d, 1 - x], cross.at[d], c_send.at[d], c_recv.at[d], "ctx", pair)

    def up_copy(d):
        return send(part.at[d, x], below.at[d], p_send.at[d], b_recv.at[d], "ctx", me + 2)

    def down_copy(d):
        return send(part.at[d, x], above.at[d], p_send.at[d], a_recv.at[d], "ctx", me - 2)

    way = 2 * lax.div(z, n // 2) - 1

    def unit_at(i):
        return lax.rem(z + way * (1 + i) + 2 * n, n)

    def take_cross(d):
        cross_copy(d).wait_recv()
        merge(rows, (part, (d, x)), (cross, (d,)), (part, (d, x)))

    def collect(r):
        def from_below():
            d = n - 1 - r + z
            send(part.at[d, x], below.at[d], p_send.at[d], b_recv.at[d], "ctx", pair).wait_recv()
            merge(rows, (part, (d, x)), (below, (d,)), (part, (d, x)))
            pl.when(d > z)(lambda: up_copy(d).start())

        def from_above():
            d = r - (n - 1) + z
            send(part.at[d, x], above.at[d], p_send.at[d], a_recv.at[d], "ctx", pair).wait_recv()
            merge(rows, (part, (d, x)), (above, (d,)), (part, (d, x)))
            pl.when(d < z)(lambda: down_copy(d).start())

        pl.when((z > 0) & (r >= z))(from_below)
        pl.when((z < n - 1) & (r + z >= n - 1))(from_above)

    def decode_step(i, carry):
        d = unit_at(i)
        peaks = [decode_scores(dims, d * 2 + t, q_ref, ck, sk_ref, s_ref.at[t]) for t in range(2)]
        for t in range(2):
            m, l, acc = decode_values(dims, d * 2 + t, peaks[t], cv, sv_ref, s_ref.at[t])
            part[d, t, :rows, :] = acc
            part[d, t, rows:, :] = pack_stats(m, l, rows)
        cross_copy(d).start()

        @pl.when(i >= 1)
        def _():
            before = unit_at(i - 1)
            take_cross(before)
            pl.when(z == 0)(lambda: up_copy(before).start())
            pl.when(z == n - 1)(lambda: down_copy(before).start())

        @pl.when(i == 0)
        def _():
            gathers[0].forward_pair()

        @pl.when((i >= 1) & (i < n - 1))
        def _():
            gathers[0].forward(pair, i)

        @pl.when(i < n - 1)
        def _():
            gathers[0].forward(me, i + 1)

        @pl.when(i == n - 2)
        def _():
            collect(1)

        @pl.when(i == 1)
        def _():
            for g in gathers[1:]:
                g.start()

        return carry

    lax.fori_loop(0, n, decode_step, 0)

    def prefill(b, p):
        prefill_unit(pre_dims, me * qblk + b, b, p, lists_ref, sq, kv[p], kc, vc, pre_s, out_v)
        if p == kvh - 1:
            span_copy(b).start()

    def span_copy(b):
        where = pl.ds(b * BLOCK, BLOCK)
        return pltpu.make_async_copy(out_v.at[where], span_hbm.at[where], out_sem.at[b])

    slots = [
        pltpu.make_async_copy(ak, ak_hbm, out_sem.at[qblk]),
        pltpu.make_async_copy(av, av_hbm, out_sem.at[qblk + 1]),
    ]

    def attended():
        merge(rows, (part, (z, x)), (fresh, ()), (fresh, ()))
        for i in range(max(1, rows // 128)):
            size = min(rows, 128)
            _, l = unpack_slab(fresh[rows + i * 8 : rows + i * 8 + 8, :])
            done = (fresh[i * 128 : i * 128 + size, :] * spread(1.0 / l, rows)).astype(bf16)
            for g in range(size // samples):
                head = i * (128 // samples) + g
                att[me, :, head * HD : (head + 1) * HD] = done[g * samples : (g + 1) * samples]

    columns = w.shape[1] // n_head
    depth = per * HD

    def att_copy(index, owner, to):
        view = att.at[owner]
        return send(view, view, t_send.at[index], t_recv.at[owner], "ctx", to)

    def line_at(j):
        return lax.rem(z - j + n, n) * 2

    def att_start():
        att_copy(0, me, pair).start()
        for j in range(1, n):
            att_copy(j, me, lax.rem(z + j, n) * 2 + x).start()

    def head_copies(index):
        bit = bits[index]
        return [
            (j, send(hpart.at[j], htook.at[j], h_send.at[j], h_recv.at[j], "head", flip(hme, bit)))
            for j in range(bit, n_head, 2 * bit)
        ]

    def terms(owner, first=False, last=False):
        order = sorted(range(n_head), key=lambda j: [1 - (j & bit) // bit for bit in bits])
        starts = dict(head_copies(0)) if last else {}
        for j in order:
            chunk = hme
            for bit in bits:
                if j & bit:
                    chunk = flip(chunk, bit)
            where = pl.ds(pl.multiple_of(chunk * columns, 128), columns)
            x = dot(att[owner], w[pl.ds(pl.multiple_of(owner * depth, 128), depth), where])
            hpart[j] = x if first else hpart[j] + x
            if j in starts:
                starts[j].start()

    def att_forward(j):
        owner = line_at(j) + x
        att_copy(0, owner, pair).wait_recv()
        att_copy(n - 1 + j, owner, pair).start()

    def project():
        loads[8].wait()
        terms(me, first=True)

        def straight(j):
            terms(line_at(j) + x)

        def paired(j):
            owner = line_at(j) + 1 - x
            att_copy(0, owner, pair).wait_recv()
            terms(owner)

        repeat(1, n, straight)
        repeat(0, n - 1, paired)
        owner = line_at(n - 1) + 1 - x
        att_copy(0, owner, pair).wait_recv()
        terms(owner, last=True)

    def halve(index):
        for j, copy in head_copies(index):
            copy.wait_recv()
            hpart[j - bits[index]] = hpart[j - bits[index]] + htook[j]
        if index + 1 < len(bits):
            for _, copy in head_copies(index + 1):
                copy.start()

    def out_copies(index):
        bit = bits[index]
        return [
            send(hout.at[j], hout.at[j + bit], o_send.at[j + bit], o_recv.at[j + bit], "head", flip(hme, bit))
            for j in range(0, n_head, 2 * bit)
        ]

    repeat(2, n - 1, collect)
    gathers[0].forward(pair, n - 1)
    for g in gathers[1:]:
        g.forward(me, 1)
    repeat(max(2, n - 1), n, collect)
    take_cross(z)
    attended()
    att_start()
    for g in gathers[1:]:
        repeat(2, n - 1, lambda s: g.forward(me, s))
    loads[7].wait()
    for b in range(qblk):
        prefill(b, 0)
        if b == 0:
            repeat(1, n - 1, att_forward)
            att_forward(n - 1)
            for g in gathers[1:]:
                g.forward(me, n - 1)
            project()
    halve(0)
    for g in gathers[1:]:
        g.finish()
    rest = [(b, p) for p in range(1, kvh) for b in range(qblk)]
    for b, p in rest[:1]:
        prefill(b, p)
    for index in range(1, len(bits)):
        halve(index)
    hout[0] = hpart[0].astype(bf16)
    for index in reversed(range(len(bits))):
        for copy in out_copies(index):
            copy.start()
        if index == len(bits) - 1:
            for b, p in rest[1:]:
                prefill(b, p)
        if index == 0:
            append_all(me, qblk, owners_ref, kv, ak, av)
            for copy in slots:
                copy.start()
        for copy in out_copies(index):
            copy.wait_recv()
    for j in range(n_head):
        chunk = hme
        for bit in bits:
            if j & bit:
                chunk = flip(chunk, bit)
        sample_ref[:, pl.ds(pl.multiple_of(chunk * columns, 128), columns)] = hout[j]

    for g in gathers:
        g.drain()

    def sent(d):
        cross_copy(d).wait_send()
        pl.when(d != z)(lambda: send(part.at[d, x], below.at[d], p_send.at[d], b_recv.at[d], "ctx", pair).wait_send())

    repeat(0, n, sent)
    for j in range(n):
        att_copy(j, me, pair).wait_send()
    for j in range(1, n):
        att_copy(n - 1 + j, line_at(j) + x, pair).wait_send()
    for index in range(len(bits)):
        for _, copy in head_copies(index):
            copy.wait_send()
        for copy in out_copies(index):
            copy.wait_send()
    for b in range(qblk):
        span_copy(b).wait()
    for copy in slots:
        copy.wait()


VM = pl.BlockSpec(memory_space=pltpu.VMEM)
SM = pl.BlockSpec(memory_space=pltpu.SMEM)
ANY = pl.BlockSpec(memory_space=pl.ANY)


def hand_over_kernel(*refs):
    count = len(refs) // 2
    for i in range(count):
        refs[count + i][...] = refs[i][...]


def hand_over(arrays):
    steps = 2
    specs = [pl.BlockSpec((a.shape[0] // steps, a.shape[1]), lambda i: (i, 0)) for a in arrays]
    return pl.pallas_call(
        hand_over_kernel,
        grid=(steps,),
        out_shape=tuple(jax.ShapeDtypeStruct(a.shape, a.dtype) for a in arrays),
        in_specs=specs,
        out_specs=tuple(specs),
        name="hand_over",
    )(*arrays)


def local(n_ctx, n_head, span_query, span_key, span_value, block_lists, owners, cache_key, cache_value, sample_query, sample_key, sample_value, out_weight):
    tokens = span_query.shape[0]
    kvh = span_key.shape[1] // HD
    group = span_query.shape[1] // HD // kvh
    qblk = tokens // BLOCK
    samples = sample_query.shape[0]
    per = kvh * group // n_ctx
    rows = per * samples
    resident = cache_key.shape[0]
    ksel = block_lists.shape[1]
    width = (ksel + 1) * BLOCK
    wide = kvh * HD
    columns = out_weight.shape[1] // n_head
    packet = rows + 8 * max(1, rows // 128)
    heads = 4
    n = n_ctx // 2
    slots = jax.ShapeDtypeStruct((MOST_BLOCKS * BLOCK, wide), bf16)
    dma = pltpu.SemaphoreType.DMA
    vm = pltpu.VMEM
    results = pl.pallas_call(
        functools.partial(layer_kernel, n_ctx, n_head, (samples, group, per, 512), (qblk, group, ksel, heads)),
        out_shape=(
            jax.ShapeDtypeStruct(span_query.shape, bf16),
            jax.ShapeDtypeStruct((samples, out_weight.shape[1]), bf16),
            slots,
            slots,
        ),
        in_specs=[SM, SM] + [ANY] * 11,
        out_specs=(ANY, VM, ANY, ANY),
        scratch_shapes=[
            vm(sample_query.shape, bf16),
            vm(span_key.shape, bf16),
            vm(span_value.shape, bf16),
            vm(sample_key.shape, bf16),
            vm(sample_value.shape, bf16),
            vm(cache_key.shape, bf16),
            vm(cache_value.shape, bf16),
            vm(span_query.shape, bf16),
            vm(out_weight.shape, bf16),
            [vm((n_ctx, 2, qblk, BLOCK, HD), bf16) for _ in range(kvh)],
            vm((2, rows, resident + tokens), f32),
            vm((group // heads, heads * BLOCK, width), f32),
            vm((width, 2 * HD), bf16),
            vm((width, HD), bf16),
            vm(span_query.shape, bf16),
            vm(slots.shape, bf16),
            vm(slots.shape, bf16),
            vm((n, 2, packet, HD), f32),
            vm((n, packet, HD), f32),
            vm((n, packet, HD), f32),
            vm((n, packet, HD), f32),
            vm((packet, HD), f32),
            vm((n_ctx, samples, per * HD), bf16),
            vm((n_head, samples, columns), f32),
            vm((n_head, samples, columns), f32),
            vm((n_head, samples, columns), bf16),
            dma((9 + 2 * kvh,)),
            dma((qblk + 2,)),
            [dma((3, n_ctx)) for _ in range(kvh)],
            [dma((n_ctx,)) for _ in range(kvh)],
            dma((n,)),
            dma((n,)),
            dma((n,)),
            dma((n,)),
            dma((n,)),
            dma((2 * n,)),
            dma((n_ctx,)),
            dma((n_head,)),
            dma((n_head,)),
            dma((n_head,)),
            dma((n_head,)),
        ],
        compiler_params=pltpu.CompilerParams(
            vmem_limit_bytes=60 << 20, collective_id=0, has_side_effects=True
        ),
        name="layer",
    )(
        block_lists.T,
        owners,
        sample_query,
        span_key,
        span_value,
        sample_key,
        sample_value,
        span_key.reshape(qblk, BLOCK, wide),
        span_value.reshape(qblk, BLOCK, wide),
        cache_key,
        cache_value,
        span_query,
        out_weight,
    )
    return hand_over(results)


def solution(mesh):
    c = P("ctx", "head")
    return jax.shard_map(
        functools.partial(local, mesh.shape["ctx"], mesh.shape["head"]),
        mesh=mesh,
        in_specs=(c, c, c, P(), P(), c, c, P(None, "head"), P(None, "head"), P(None, "head"), P("head", "ctx")),
        out_specs=(c, P(None, "ctx"), c, c),
        check_vma=False,
    )
```
